128 devices in a mesh: branch: 4 (over z_hi, core), seq: 8 (over z_lo, x), rep: 4 (over y).
Axes of the slice: x: 4, y: 4, z: 4 (z_hi: 2, z_lo: 2; z = z_hi * 2 + z_lo), core: 2. Of those that a mesh axis runs over, the one named last changes fastest.
Arguments:
- noisy: bfloat16 [4, 1024, 5120], P('rep'), may hold values from -6 to 6
- generated: bfloat16 [4, 1024, 5120], P('rep', 'seq'), may hold values from -170 to 170
- caption: bfloat16 [4, 5120], P('rep'), may hold values from -0.59765625 to 0.59765625
- null_caption: bfloat16 [5120], replicated, may hold values from -0.59765625 to 0.59765625
- caption_drop: int32 [4], P('rep'), may hold values from 0 to 1, as said below
- timestep: int32 [4], P('rep'), may hold values from 0 to 999
- window_start: int32 [4], P('rep'), may hold values from 0 to 31736
- teacher_qkv: bfloat16 [3, 5120, 4096], P(None, None, ('branch', 'seq')), may hold values from -0.078125 to 0.078125
- teacher_out: bfloat16 [4096, 5120], P(('branch', 'seq')), may hold values from -0.09375 to 0.09375
- teacher_gain: float32 [5120], replicated, may hold values from 0.5 to 1.5
- teacher_qk_gain: float32 [2, 4096], P(None, ('branch', 'seq')), may hold values from 0.7 to 2.6
- critic_qkv: bfloat16 [3, 5120, 4096], P(None, None, ('branch', 'seq')), may hold values from -0.078125 to 0.078125
- critic_out: bfloat16 [4096, 5120], P(('branch', 'seq')), may hold values from -0.09375 to 0.09375
- critic_gain: float32 [5120], replicated, may hold values from 0.5 to 1.5
- critic_qk_gain: float32 [2, 4096], P(None, ('branch', 'seq')), may hold values from 0.7 to 2.6
Outputs:
- generator_grad: bfloat16 [4, 1024, 5120], P('rep', 'seq')
- critic_qkv_grad: float32 [3, 5120, 4096], P(None, 'rep', ('branch', 'seq'))
- critic_out_grad: float32 [4096, 5120], P(('branch', 'seq'), 'rep')
The draws below stay inside these ranges and needn't reach their ends.
Inputs may be any that keep to these rules, and one draw needn't show every extreme that they name: `caption_drop`: each window's flag is drawn independently.
All inputs are finite; a program needn't handle non-finite values. Where the reference program divides by a largest or mean magnitude, that divisor is 1e-20 or more.
Results may differ from the reference program's by a relative error of at most 0.018.
The reference program's roundings to bfloat16 on the way count: a program that leaves them out, or rounds other values in their place, can miss the bound.
Values may be sent and summed in bfloat16 or wider, within the bound.
A program may use at most 192 MiB of HBM per device.

```python
import math
import jax
import jax.numpy as jnp
from jax import lax

D = 5120
HEAD = 128
HEADS_DEV = 1
LEN = 1024
FRAMES = 21
GRID_H = 30
GRID_W = 52
H = 32
HT = 4096
SAMPLES = 4


def draw_generated(key, part):
    base_key = jax.random.fold_in(key, 11)
    key_list = jax.random.split(base_key, 3)
    base = jnp.clip(jax.random.normal(key_list[0], (SAMPLES, LEN, D), jnp.float32), -5.0, 5.0)
    rising = jnp.exp(jnp.log(3.0) * jnp.arange(LEN, dtype=jnp.float32) / (LEN - 1.0))
    row_scale = jnp.exp(jax.random.uniform(key_list[1], (SAMPLES, LEN, 1), jnp.float32, 0.0, jnp.log(10.0)))
    column_scale = jnp.exp(jax.random.uniform(key_list[2], (1, 1, D), jnp.float32, 0.0, jnp.log(10.0)))
    return (base * row_scale * column_scale * rising[None, :, None] / 16.0).astype(jnp.bfloat16)


def draw_caption_drop(key, part):
    drop_key = jax.random.fold_in(key, 23)
    return jax.random.randint(drop_key, (SAMPLES,), 0, 2, jnp.int32)


def place_ends(array, rng, least, high):
    shape = array.shape
    spot = [jax.random.randint(jax.random.fold_in(rng, axis), (), 0, shape[axis]) for axis in range(len(shape))]
    array = array.at[tuple(spot)].set(least)
    longest = shape.index(max(shape))
    spot[longest] = (spot[longest] + 1) % shape[longest]
    return array.at[tuple(spot)].set(high)


def steps_of(own_key, dims, cuts, low, largest):
    def one(position, blocks):
        heights = jax.random.uniform(jax.random.fold_in(jax.random.fold_in(own_key, 6), position), (blocks,), jnp.float32, low / len(cuts), largest / len(cuts))
        return jnp.repeat(jnp.exp(heights), dims[position] // blocks).reshape((-1,) + (1,) * (len(dims) - position - 1))

    gain = one(*cuts[0])
    for cut in cuts[1:]:
        gain = gain * one(*cut)
    return gain


def scatter_about(stream_key, shape, width, reach, shards=(), held_as=jnp.bfloat16):
    result = jax.random.normal(stream_key, shape, jnp.float32) * width
    if len(shards) > 0:
        result = steps_of(stream_key, shape, shards, -0.22, 0.18) * result
    return jnp.clip(result, min=-reach, max=reach).astype(held_as)


def setup_inputs(seed: int = 0) -> dict:
    streams_of = jax.random.split(jax.random.key(seed), 16)
    return {
        "noisy": scatter_about(streams_of[0], (SAMPLES, LEN, D), 1.0, 6.0, ((0, 4),)),
        "generated": draw_generated(jax.random.fold_in(streams_of[15], 71), 0),
        "caption": scatter_about(streams_of[2], (SAMPLES, D), 0.1, 0.59765625, ((0, 4),)),
        "null_caption": scatter_about(streams_of[3], (D,), 0.1, 0.59765625),
        "caption_drop": draw_caption_drop(jax.random.fold_in(streams_of[15], 71), 0),
        "timestep": place_ends(jax.random.randint(streams_of[5], (SAMPLES,), 0, 1000), jax.random.fold_in(streams_of[5], 1), 0, 999).astype(jnp.int32),
        "window_start": place_ends(jax.random.randint(streams_of[6], (SAMPLES,), 0, FRAMES * GRID_H * GRID_W - LEN + 1), jax.random.fold_in(streams_of[6], 1), 0, FRAMES * GRID_H * GRID_W - LEN).astype(jnp.int32),
        "teacher_qkv": scatter_about(streams_of[7], (3, D, HT), D ** -0.5, 0.078125, ((2, 32),)),
        "teacher_out": scatter_about(streams_of[8], (HT, D), HT ** -0.5, 0.09375, ((0, 32),)),
        "teacher_gain": jnp.clip(1.0 + 0.1 * jax.random.normal(streams_of[9], (D,), jnp.float32), 0.5, 1.5),
        "teacher_qk_gain": jnp.clip(jnp.exp(math.log(2.6) - 1.3121864 * jax.random.uniform(streams_of[10], (2, HT), jnp.float32) ** steps_of(streams_of[10], (2, HT), ((1, 32),), -0.2, 0.2)), 0.7, 2.6),
        "critic_qkv": scatter_about(streams_of[11], (3, D, HT), D ** -0.5, 0.078125, ((2, 32),)),
        "critic_out": scatter_about(streams_of[12], (HT, D), HT ** -0.5, 0.09375, ((0, 32),)),
        "critic_gain": jnp.clip(1.0 + 0.1 * jax.random.normal(streams_of[13], (D,), jnp.float32), 0.5, 1.5),
        "critic_qk_gain": jnp.clip(jnp.exp(math.log(2.6) - 1.3121864 * jax.random.uniform(streams_of[14], (2, HT), jnp.float32) ** steps_of(streams_of[14], (2, HT), ((1, 32),), -0.2, 0.2)), 0.7, 2.6),
    }


guidance = 5.0
score_scale = 128.0 ** (-0.5)
norm_eps = 1e-06

def rounded(values):
    return lax.optimization_barrier(values.astype(jnp.bfloat16))

def rope_tables(first_token):
    token_index = first_token + jnp.arange(LEN, dtype=jnp.int32)
    plane_size = GRID_H * GRID_W
    frame_index = token_index // plane_size
    remainder = token_index - frame_index * plane_size
    row_index = remainder // GRID_W
    column_index = remainder - row_index * GRID_W
    pair_index = jnp.arange(64, dtype=jnp.int32)
    in_frames = pair_index < 22
    in_rows = jnp.logical_and(pair_index >= 22, pair_index < 43)
    local_rank = jnp.where(in_frames, pair_index, jnp.where(in_rows, pair_index - 22, pair_index - 43)).astype(jnp.float32)
    axis_width = jnp.where(in_frames, 44.0, 42.0).astype(jnp.float32)
    frequency = jnp.exp(-jnp.log(10000.0) * 2.0 * local_rank / axis_width)
    chosen = jnp.where(in_frames[None, :], frame_index[:, None], jnp.where(in_rows[None, :], row_index[:, None], column_index[:, None])).astype(jnp.float32)
    angles = chosen * frequency[None, :]
    angles = jnp.concatenate([angles, angles], axis=1)
    return (jnp.cos(angles), jnp.sin(angles))

def rotate_half(values):
    return jnp.concatenate([-values[..., 64:], values[..., :64]], axis=-1)

def rotate_back(values):
    return jnp.concatenate([values[..., 64:], -values[..., :64]], axis=-1)

def norm_tokens(inputs, gain_values):
    scaled = inputs * lax.rsqrt(lax.optimization_barrier(jnp.mean(inputs * inputs, axis=-1, keepdims=True)) + norm_eps) * gain_values
    return rounded(scaled)

def undo_norm(raw_values, inverse, gain_values, grad_normed):
    scaled = gain_values * grad_normed
    return inverse * scaled - raw_values * inverse * inverse * inverse * lax.optimization_barrier(jnp.mean(scaled * raw_values, axis=-1, keepdims=True))

def head_forward(hidden, weights, qk_gains, cosine_table, sine_table):
    projected = jnp.einsum('sd,kdc->ksc', hidden.astype(jnp.float32), weights.astype(jnp.float32))
    length = hidden.shape[0]
    query_raw = projected[0].reshape(length, -1, 128)
    key_raw = projected[1].reshape(length, -1, 128)
    value_rows = rounded(projected[2].reshape(length, -1, 128))
    gain_query = qk_gains[0].reshape(-1, 128)
    gain_key = qk_gains[1].reshape(-1, 128)
    inv_query = lax.rsqrt(lax.optimization_barrier(jnp.mean(query_raw * query_raw, axis=-1, keepdims=True)) + norm_eps)
    inv_key = lax.rsqrt(lax.optimization_barrier(jnp.mean(key_raw * key_raw, axis=-1, keepdims=True)) + norm_eps)
    normed_query = query_raw * inv_query * gain_query
    normed_key = key_raw * inv_key * gain_key
    cosine_h = cosine_table[:, None, :]
    sine_h = sine_table[:, None, :]
    rope_query = rounded(normed_query * cosine_h + rotate_half(normed_query) * sine_h)
    rope_key = rounded(normed_key * cosine_h + rotate_half(normed_key) * sine_h)
    scores = jnp.einsum('qhe,khe->hqk', rope_query.astype(jnp.float32), rope_key.astype(jnp.float32)) * score_scale
    exponent = jnp.exp(scores)
    probability = exponent / lax.optimization_barrier(jnp.sum(exponent, axis=-1, keepdims=True))
    prob_rounded = rounded(probability)
    attended = jnp.einsum('hqk,khe->qhe', prob_rounded.astype(jnp.float32), value_rows.astype(jnp.float32))
    attended = rounded(attended).reshape(length, -1)
    saved_state = (query_raw, key_raw, inv_query, inv_key, rope_query, rope_key, value_rows, probability, prob_rounded)
    return (attended, saved_state)

def head_backward(hidden, grad_attn, saved_state, qk_gains, cosine_table, sine_table):
    query_raw, key_raw, inv_query, inv_key, rope_query, rope_key, value_rows, probability, prob_rounded = saved_state
    length = hidden.shape[0]
    grad_heads = grad_attn.reshape(length, -1, 128).astype(jnp.float32)
    grad_prob = jnp.einsum('qhe,khe->hqk', grad_heads, value_rows.astype(jnp.float32))
    grad_score = probability * (grad_prob - lax.optimization_barrier(jnp.sum(grad_prob * probability, axis=-1, keepdims=True))) * score_scale
    grad_score = rounded(grad_score).astype(jnp.float32)
    grad_qrot = jnp.einsum('hqk,khe->qhe', grad_score, rope_key.astype(jnp.float32))
    grad_krot = jnp.einsum('hqk,qhe->khe', grad_score, rope_query.astype(jnp.float32))
    grad_value = jnp.einsum('hqk,qhe->khe', prob_rounded.astype(jnp.float32), grad_heads)
    cosine_h = cosine_table[:, None, :]
    sine_h = sine_table[:, None, :]
    grad_qnorm = grad_qrot * cosine_h + rotate_back(grad_qrot * sine_h)
    grad_knorm = grad_krot * cosine_h + rotate_back(grad_krot * sine_h)
    grad_query = undo_norm(query_raw, inv_query, qk_gains[0].reshape(-1, 128), grad_qnorm)
    grad_key = undo_norm(key_raw, inv_key, qk_gains[1].reshape(-1, 128), grad_knorm)
    grad_stack = rounded(jnp.stack([grad_query.reshape(length, -1), grad_key.reshape(length, -1), grad_value.reshape(length, -1)]))
    return jnp.einsum('sd,ksc->kdc', hidden.astype(jnp.float32), grad_stack.astype(jnp.float32))

def reference(noisy, generated, caption, null_caption, caption_drop, timestep, window_start, teacher_qkv, teacher_out, teacher_gain, teacher_qk_gain, critic_qkv, critic_out, critic_gain, critic_qk_gain):
    group_width = HEAD * HEADS_DEV
    group_total = H // HEADS_DEV
    group_ids = jnp.arange(group_total, dtype=jnp.int32)

    def one_sample(totals, sample_data):
        latent_row, target_row, caption_row, drop_flag, step_index, first_token = sample_data
        fraction = (step_index.astype(jnp.float32) + 1.0) / 1001.0
        noise_level = 5.0 * fraction / (1.0 + 4.0 * fraction)
        used_caption = jnp.where(drop_flag == 1, null_caption, caption_row)
        latent = latent_row.astype(jnp.float32)
        cond_input = latent + used_caption.astype(jnp.float32)[None, :]
        null_input = latent + null_caption.astype(jnp.float32)[None, :]
        cond_normed = norm_tokens(cond_input, teacher_gain)
        null_normed = norm_tokens(null_input, teacher_gain)
        critic_normed = norm_tokens(cond_input, critic_gain)
        cosine_table, sine_table = rope_tables(first_token)

        def slices(group_id):
            first_col = (group_id * group_width).astype(jnp.int32)
            return (lax.dynamic_slice_in_dim(teacher_qkv, first_col, group_width, 2), lax.dynamic_slice_in_dim(teacher_qk_gain, first_col, group_width, 1), lax.dynamic_slice_in_dim(teacher_out, first_col, group_width, 0), lax.dynamic_slice_in_dim(critic_qkv, first_col, group_width, 2), lax.dynamic_slice_in_dim(critic_qk_gain, first_col, group_width, 1), lax.dynamic_slice_in_dim(critic_out, first_col, group_width, 0))

        def forward_group(running, group_id):
            teacher_cols, teacher_gains, teacher_rows, critic_cols, critic_gains, critic_rows = slices(group_id)
            cond_attn, unused = head_forward(cond_normed, teacher_cols, teacher_gains, cosine_table, sine_table)
            null_attn, unused = head_forward(null_normed, teacher_cols, teacher_gains, cosine_table, sine_table)
            fake_attn, unused = head_forward(critic_normed, critic_cols, critic_gains, cosine_table, sine_table)
            cond_part = jnp.dot(cond_attn, teacher_rows, preferred_element_type=jnp.float32)
            null_part = jnp.dot(null_attn, teacher_rows, preferred_element_type=jnp.float32)
            fake_part = jnp.dot(fake_attn, critic_rows, preferred_element_type=jnp.float32)
            guided_term = rounded(guidance * cond_part - (guidance - 1.0) * null_part).astype(jnp.float32)
            fake_term = rounded(fake_part).astype(jnp.float32)
            return ((running[0] + guided_term, running[1] + fake_term), None)
        empty_sum = jnp.zeros((LEN, D), jnp.float32)
        (guided_sum, fake_sum), unused = lax.scan(forward_group, (empty_sum, empty_sum), group_ids)
        real_velocity = guidance * cond_input - (guidance - 1.0) * null_input + guided_sum
        fake_velocity = cond_input + fake_sum
        real_pred = latent - noise_level * real_velocity
        fake_pred = latent - noise_level * fake_velocity
        target = target_row.astype(jnp.float32)
        spread = jnp.mean(jnp.abs(real_pred - target))
        generator_grad = ((fake_pred - real_pred) / (spread + 1e-05)).astype(jnp.bfloat16)
        fake_cotangent = rounded(-noise_level * (fake_pred - target) / 64.0)

        def backward_group(carried, group_id):
            teacher_cols, teacher_gains, teacher_rows, critic_cols, critic_gains, critic_rows = slices(group_id)
            fake_attn, saved_state = head_forward(critic_normed, critic_cols, critic_gains, cosine_table, sine_table)
            out_part = jnp.dot(fake_attn.T, fake_cotangent, preferred_element_type=jnp.float32)
            grad_attn = rounded(jnp.dot(fake_cotangent, critic_rows.T, preferred_element_type=jnp.float32))
            proj_part = head_backward(critic_normed, grad_attn, saved_state, critic_gains, cosine_table, sine_table)
            return (carried, (proj_part, out_part))
        carried, (proj_parts, out_parts) = lax.scan(backward_group, jnp.zeros((), jnp.float32), group_ids)
        proj_grads = jnp.transpose(proj_parts, (1, 2, 0, 3)).reshape(3, D, HT)
        out_grads = out_parts.reshape(HT, D)
        return ((totals[0] + proj_grads, totals[1] + out_grads), generator_grad)
    start_totals = (jnp.zeros((3, D, HT), jnp.float32), jnp.zeros((HT, D), jnp.float32))
    (proj_total, out_total), generator_grad = lax.scan(one_sample, start_totals, (noisy, generated, caption, caption_drop, timestep, window_start))
    return (generator_grad, proj_total, out_total)
```

```python
import jax
import jax.numpy as jnp
from jax import lax
from jax.experimental import pallas as pl
from jax.experimental.pallas import tpu as pltpu
from jax.sharding import PartitionSpec as P

LEN = 1024
GRID_H = 30
GRID_W = 52
D = 5120
HEAD = 128
NB = 32
ROWS = 256
COLS = 640
NR = LEN // ROWS
PAD = 16
BLK = ROWS + PAD
FEAT = 1280

guidance = 5.0
score_scale = 128.0 ** (-0.5)
norm_eps = 1e-06
f32 = jnp.float32
bf16 = jnp.bfloat16
MESH = pl.DeviceIdType.MESH


def rope_tables(first_token):
    token_index = first_token + jnp.arange(LEN, dtype=jnp.int32)
    plane_size = GRID_H * GRID_W
    frame_index = token_index // plane_size
    remainder = token_index - frame_index * plane_size
    row_index = remainder // GRID_W
    column_index = remainder - row_index * GRID_W
    pair_index = jnp.arange(64, dtype=jnp.int32)
    in_frames = pair_index < 22
    in_rows = jnp.logical_and(pair_index >= 22, pair_index < 43)
    local_rank = jnp.where(
        in_frames, pair_index, jnp.where(in_rows, pair_index - 22, pair_index - 43)
    ).astype(f32)
    axis_width = jnp.where(in_frames, 44.0, 42.0).astype(f32)
    frequency = jnp.exp(-jnp.log(10000.0) * 2.0 * local_rank / axis_width)
    chosen = jnp.where(
        in_frames[None, :],
        frame_index[:, None],
        jnp.where(in_rows[None, :], row_index[:, None], column_index[:, None]),
    ).astype(f32)
    angles = chosen * frequency[None, :]
    cosine = jnp.cos(angles)
    sine = jnp.sin(angles)
    return (
        jnp.concatenate([cosine, cosine], axis=1),
        jnp.concatenate([-sine, sine], axis=1),
    )


def dot(a, b):
    return jnp.dot(a, b, preferred_element_type=f32)


def dot_nt(a, b):
    return lax.dot_general(a, b, (((1,), (1,)), ((), ())), preferred_element_type=f32)


def dot_tn(a, b):
    return lax.dot_general(a, b, (((0,), (0,)), ((), ())), preferred_element_type=f32)


def half_turn(x):
    return pltpu.roll(x, 64, 1)


def step_kernel(
    noisy_h, wc_h, wt_h, caps_h, cos_h, sin_h, cqk, tqk, level, caps, cgain, gen_h, cout_h, tout_h,
    gg_h, qg_h, og_h, ogin_h,
    noisy, wcx, wtx, ac, ag, gain_in, qgin, og8in, diff_in, abs_in, gen, cos, sin,
    qraw, kraw, qr, kr, vv, rc, rn, invq, invk, linv, fa, gt,
    lsem, rsem, ssem,
):
    b = lax.axis_index("branch")
    s = lax.axis_index("seq")
    w = lax.axis_index("rep")
    me = b * 8 + s
    myc = b * 2 + lax.rem(s, 2)
    myr = s // 2

    def plane(q):
        return {"branch": q // 8, "seq": lax.rem(q, 8)}

    def col_of(q):
        return (q // 8) * 2 + lax.rem(q, 2)

    def row_of(q):
        return lax.rem(q, 8) // 2

    def peer(k):
        return lax.rem(me + k, NB)

    EW, EG, ET, EA, EU, EB, EO, ED, ES, EQ, E8 = range(11)

    def send(src, dst, e, device):
        pltpu.make_async_remote_copy(
            src_ref=src, dst_ref=dst, send_sem=ssem.at[e], recv_sem=rsem.at[e],
            device_id=device, device_id_type=MESH,
        ).start()

    def local(src, dst, sem):
        c = pltpu.make_async_copy(src, dst, sem)
        c.start()
        return c

    def wait_bytes(ref, sem):
        pltpu.make_async_copy(ref, ref, sem).wait()

    for i in range(NR):
        local(noisy_h.at[pl.ds(i * ROWS, ROWS), :], noisy.at[i, pl.ds(0, ROWS), :], lsem.at[i])
    cap_copies = [local(caps_h, noisy.at[i, pl.ds(ROWS, PAD), :], lsem.at[4 + i]) for i in range(NR)]
    cos_copy = local(cos_h, cos, lsem.at[8])
    sin_copy = local(sin_h, sin, lsem.at[9])

    barrier = pltpu.get_barrier_semaphore()

    @pl.loop(1, NB)
    def _(k):
        pl.semaphore_signal(barrier, inc=1, device_id=plane(peer(k)), device_id_type=MESH)

    for k in range(1, 4):
        pl.semaphore_signal(
            barrier, inc=1, device_id={"rep": lax.rem(w + k, 4)}, device_id_type=MESH
        )
    pl.semaphore_wait(barrier, NB - 1 + 3)

    def weights(src, dst, e):
        mine = dst.at[pl.ds(me * HEAD, HEAD), :]

        @pl.loop(1, NB)
        def _(k):
            q = peer(k)
            send(src.at[:, pl.ds(pl.multiple_of(col_of(q) * COLS, COLS), COLS)], mine, e, plane(q))

        local(src.at[:, pl.ds(pl.multiple_of(myc * COLS, COLS), COLS)], mine, rsem.at[e])

    weights(cout_h, wcx, EW)
    partner = me + 1 - 2 * lax.rem(s, 2)
    gen_rows = gen.at[pl.ds(pl.multiple_of(lax.rem(s, 2) * 128, 128), 128), :]
    send(
        gen_h.at[:, pl.ds(pl.multiple_of(col_of(partner) * COLS, COLS), COLS)],
        gen_rows, EG, plane(partner),
    )
    local(gen_h.at[:, pl.ds(pl.multiple_of(myc * COLS, COLS), COLS)], gen_rows, rsem.at[EG])

    def tokens(src, dst, e):
        mine = dst.at[:, pl.ds(pl.multiple_of(me * HEAD, HEAD), HEAD)]

        @pl.loop(1, NB)
        def _(k):
            q = peer(k)
            send(src.at[pl.ds(pl.multiple_of(row_of(q) * ROWS, ROWS), ROWS), :], mine, e, plane(q))

        local(src.at[pl.ds(pl.multiple_of(myr * ROWS, ROWS), ROWS), :], mine, rsem.at[e])

    def forward_phase(wall, pbuf, att_a):
        def load_w(j):
            src = wc_h if j < 3 else wt_h
            return local(src.at[j % 3], wall.at[:, pl.ds(j * HEAD, HEAD)], lsem.at[10 + j])

        w_copies = [load_w(j) for j in range(6)]

        for c in cap_copies:
            c.wait()
        for c in w_copies[:4]:
            c.wait()

        @pl.loop(0, NR)
        def _(i):
            pltpu.make_async_copy(
                noisy_h.at[pl.ds(i * ROWS, ROWS), :], noisy.at[i, pl.ds(0, ROWS), :], lsem.at[i]
            ).wait()
            pbuf[i, :, 0:512] = dot(noisy[i], wall[:, 0:512])
            for half in range(2):
                top = half * 128
                acc_c = jnp.zeros((128, 128), f32)
                acc_n = jnp.zeros((128, 128), f32)
                for j in range(D // 128):
                    x = noisy[i, top : top + 128, j * 128 : j * 128 + 128].astype(f32)
                    u = x + caps[0:1, j * 128 : j * 128 + 128]
                    v = x + caps[1:2, j * 128 : j * 128 + 128]
                    acc_c += u * u
                    acc_n += v * v
                sum_c = jnp.sum(acc_c, axis=1, keepdims=True) * (1.0 / D)
                sum_n = jnp.sum(acc_n, axis=1, keepdims=True) * (1.0 / D)
                rc[i, top : top + 128, :] = jnp.broadcast_to(
                    lax.rsqrt(sum_c + norm_eps), (128, 128)
                )
                rn[i, top : top + 128, :] = jnp.broadcast_to(
                    lax.rsqrt(sum_n + norm_eps), (128, 128)
                )

        cos_copy.wait()
        sin_copy.wait()

        def attention(col, row, scale_ref, gains, keep, out):
            @pl.loop(0, NR)
            def _(i):
                rows = pl.ds(pl.multiple_of(i * ROWS, ROWS), ROWS)
                scale = scale_ref[i]
                cosine = cos[rows, :]
                sine = sin[rows, :]

                def raw(m):
                    block = pbuf[i, 0:ROWS, col + m * HEAD : col + (m + 1) * HEAD]
                    shift = pbuf[
                        i, ROWS + row : ROWS + row + 1, col + m * HEAD : col + (m + 1) * HEAD
                    ]
                    return scale * (block + shift)

                for m, (dst, raw_ref, inv_ref) in enumerate(((qr, qraw, invq), (kr, kraw, invk))):
                    x = raw(m)
                    inverse = lax.rsqrt(jnp.mean(x * x, axis=1, keepdims=True) + norm_eps)
                    normed = x * inverse * gains[m : m + 1, :]
                    dst[rows, :] = (normed * cosine + half_turn(normed) * sine).astype(bf16)
                    if keep:
                        raw_ref[rows, :] = x
                        inv_ref[rows, :] = jnp.broadcast_to(inverse, (ROWS, HEAD))
                vv[rows, :] = raw(2).astype(bf16)

            @pl.loop(0, NR)
            def _(i):
                rows = pl.ds(pl.multiple_of(i * ROWS, ROWS), ROWS)
                exponent = jnp.exp(dot_nt(qr[rows, :], kr[...]) * score_scale)
                inverse = 1.0 / jnp.sum(exponent, axis=1, keepdims=True)
                if keep:
                    linv[rows, :] = jnp.broadcast_to(inverse, (ROWS, HEAD))
                prob = (exponent * inverse).astype(bf16)
                out(rows, dot(prob, vv[...]).astype(bf16))

        def to_a(rows, x):
            att_a[rows, :] = x

        def to_fake(rows, x):
            fa[rows, :] = x

        def to_guided(rows, x):
            gt[rows, :] = (
                guidance * att_a[rows, :].astype(f32) - (guidance - 1.0) * x.astype(f32)
            ).astype(bf16)

        for c in w_copies[4:]:
            c.wait()

        @pl.loop(0, NR)
        def _(i):
            pbuf[i, :, 512:768] = dot(noisy[i], wall[:, 512:768])

        attention(384, 0, rc, tqk, False, to_a)
        attention(384, 1, rn, tqk, False, to_guided)
        tokens(gt, ag, EU)
        attention(0, 0, rc, cqk, True, to_fake)
        tokens(fa, ac, EA)
        weights(tout_h, wtx, ET)

    pl.run_scoped(
        forward_phase,
        pltpu.VMEM((D, 6 * HEAD), bf16),
        pltpu.VMEM((NR, BLK, 6 * HEAD), f32),
        pltpu.VMEM((LEN, HEAD), bf16),
    )

    noise = level[0:1, 0:1]

    def later_phase(gaout, ogout, cot, diff_out, abs_out, qgout, qgown, ga, gk, gv, rg, rgt, og8):
        tile_cols = pl.ds(pl.multiple_of(myc * COLS, COLS), COLS)
        wait_bytes(gen, rsem.at[EG])
        wait_bytes(wcx, rsem.at[EW])
        wait_bytes(ac, rsem.at[EA])

        def predictions(i, total, guided):
            rows = pl.ds(pl.multiple_of(i * 128, 128), 128)
            latent = noisy[myr, rows, tile_cols].astype(f32)
            cond = latent + caps[0:1, tile_cols]
            if guided:
                null = latent + caps[1:2, tile_cols]
                velocity = guidance * cond - (guidance - 1.0) * null + total
            else:
                velocity = cond + total
            return latent - noise * velocity

        @pl.loop(0, 2)
        def _(i):
            rows = pl.ds(pl.multiple_of(i * 128, 128), 128)
            fake_pred = predictions(i, dot(ac[rows, :], wcx[...]), False)
            target = gen[rows, :].astype(f32)
            cot[rows, :] = (-noise * (fake_pred - target) * (1.0 / 64.0)).astype(bf16)
            diff_out[rows, :] = fake_pred

        @pl.loop(0, 8)
        def _(j):
            part = dot_nt(cot[...], wcx[pl.ds(pl.multiple_of(j * 512, 512), 512), :])
            for m in range(4):
                gaout[j * 4 + m] = part[:, m * HEAD : (m + 1) * HEAD].astype(bf16)

        def blocks(src, dst, e):
            @pl.loop(1, NB)
            def _(k):
                q = peer(k)
                send(src.at[q], dst.at[me], e, plane(q))

            local(src.at[me], dst.at[me], rsem.at[e])

        blocks(gaout, gain_in, EB)

        @pl.loop(0, 8)
        def _(j):
            part = dot_tn(ac[:, pl.ds(pl.multiple_of(j * 512, 512), 512)], cot[...])
            for m in range(4):
                ogout[j * 4 + m] = part[m * HEAD : (m + 1) * HEAD, :].astype(bf16)

        blocks(ogout, ogin_h, EO)

        wait_bytes(gain_in, rsem.at[EB])

        @pl.loop(0, NR)
        def _(i):
            total = jnp.zeros((ROWS, HEAD), f32)
            for c in range(8):
                total += gain_in[(c // 2) * 8 + i * 2 + c % 2].astype(f32)
            ga[pl.ds(pl.multiple_of(i * ROWS, ROWS), ROWS), :] = total.astype(bf16)

        gk[...] = jnp.zeros_like(gk)
        gv[...] = jnp.zeros_like(gv)

        def undo(rows, raw_ref, inv_ref, gain, grad):
            turned = grad * cos[rows, :] + half_turn(grad * sin[rows, :])
            scaled = gain * turned
            raw = raw_ref[rows, :]
            inverse = inv_ref[rows, :]
            back = inverse * scaled - raw * inverse * inverse * inverse * jnp.mean(
                scaled * raw, axis=1, keepdims=True
            )
            return back.astype(bf16).astype(f32)

        @pl.loop(0, NR)
        def _(i):
            rows = pl.ds(pl.multiple_of(i * ROWS, ROWS), ROWS)
            inverse = linv[rows, :][:, 0:1]
            prob = jnp.exp(dot_nt(qr[rows, :], kr[...]) * score_scale) * inverse
            grads = ga[rows, :]
            grad_prob = dot_nt(grads, vv[...])
            mean = jnp.sum(grad_prob * prob, axis=1, keepdims=True)
            grad_score = (prob * (grad_prob - mean) * score_scale).astype(bf16)
            gq = dot(grad_score, kr[...])
            gk[...] += dot_tn(qr[rows, :], grad_score)
            gv[...] += dot_tn(grads, prob.astype(bf16))
            rg[rows, 0:HEAD] = rc[i] * undo(rows, qraw, invq, cqk[0:1, :], gq)

        for i in range(NR):
            rows = pl.ds(i * ROWS, ROWS)
            grad_k = gk[:, i * ROWS : (i + 1) * ROWS].T
            grad_v = gv[:, i * ROWS : (i + 1) * ROWS].T
            rg[rows, HEAD : 2 * HEAD] = rc[i] * undo(rows, kraw, invk, cqk[1:2, :], grad_k)
            rg[rows, 2 * HEAD :] = rc[i] * grad_v.astype(bf16).astype(f32)

        for i in range(NR):
            for m in range(3):
                rgt[m * HEAD : (m + 1) * HEAD, i * ROWS : (i + 1) * ROWS] = (
                    rg[i * ROWS : (i + 1) * ROWS, m * HEAD : (m + 1) * HEAD].T.astype(bf16)
                )
        row_sum = jnp.sum(rgt[...].astype(f32), axis=1, keepdims=True)

        def share(target, put):
            @pl.loop(0, FEAT // 256)
            def _(j):
                cols = pl.ds(pl.multiple_of(target * FEAT + j * 256, 256), 256)
                total = row_sum * caps[0:1, cols]
                for i in range(NR):
                    total += dot(rgt[:, i * ROWS : (i + 1) * ROWS], noisy[i, 0:ROWS, cols])
                put(pl.ds(pl.multiple_of(j * 256, 256), 256), total * cgain[0:1, cols])

        for off in (2, 1, 3):
            target = lax.rem(w + off, 4)

            def put(cols, x, off=off):
                qgout[off - 1, :, cols] = x.astype(bf16)

            share(target, put)
            send(qgout.at[off - 1], qgin.at[off - 1], EQ, {"rep": target})

        def put_own(cols, x):
            qgown[:, cols] = x

        share(w, put_own)

        wait_bytes(ogin_h, rsem.at[EO])
        wait_bytes(ogout.at[pl.ds(0, NB - 1)], ssem.at[EO])
        pltpu.sync_copy(ogin_h, ogout)

        def og_share(target, put):
            for half in range(2):
                total = jnp.zeros((HEAD, COLS), f32)
                for r in range(NR):
                    total += ogout[target * 8 + r * 2 + half].astype(f32)
                put(pl.ds(half * COLS, COLS), total)

        for off in (2, 1, 3):
            target = lax.rem(w + off, 4)

            def put8(cols, x, off=off):
                og8[off - 1, :, cols] = x.astype(bf16)

            og_share(target, put8)
            send(og8.at[off - 1], og8in.at[off - 1], E8, {"rep": target})

        wait_bytes(wtx, rsem.at[ET])
        wait_bytes(ag, rsem.at[EU])
        abs_out[...] = jnp.zeros_like(abs_out)

        @pl.loop(0, 2)
        def _(i):
            rows = pl.ds(pl.multiple_of(i * 128, 128), 128)
            real_pred = predictions(i, dot(ag[rows, :], wtx[...]), True)
            target = gen[rows, :].astype(f32)
            gap = jnp.abs(real_pred - target)
            lanes = gap[:, 0:128]
            for j in range(1, COLS // 128):
                lanes += gap[:, j * 128 : (j + 1) * 128]
            eight = lanes[0:8, :]
            for j in range(1, 16):
                eight += lanes[j * 8 : (j + 1) * 8, :]
            abs_out[...] += eight
            cot[rows, :] = (diff_out[rows, :] - real_pred).astype(bf16)

        @pl.loop(1, NB)
        def _(k):
            send(abs_out, abs_in.at[me], ES, plane(peer(k)))

        local(abs_out, abs_in.at[me], rsem.at[ES])

        def diff_rows(t):
            return cot.at[pl.ds(pl.multiple_of(lax.rem(t, 2) * 128, 128), 128), :]

        diff_mine = diff_in.at[:, tile_cols]

        @pl.loop(1, 8)
        def _(k):
            t = lax.rem(myc + k, 8)
            send(
                diff_rows(t), diff_mine, ED,
                {"branch": t // 2, "seq": myr * 2 + lax.rem(t, 2)},
            )

        local(diff_rows(myc), diff_mine, rsem.at[ED])
        wait_bytes(abs_in, rsem.at[ES])
        wait_bytes(diff_in, rsem.at[ED])
        spread = jnp.sum(jnp.sum(abs_in[...], axis=0), axis=(0, 1), keepdims=True) * (
            1.0 / (LEN * D)
        )
        factor = 1.0 / (spread + 1e-05)

        @pl.loop(0, 8)
        def _(j):
            cols = pl.ds(pl.multiple_of(j * COLS, COLS), COLS)
            diff_in[:, cols] = (diff_in[:, cols].astype(f32) * factor).astype(bf16)

        gg_copy = local(diff_in, gg_h, lsem.at[17])

        wait_bytes(qgin, rsem.at[EQ])

        def sum_q(out):
            for m in range(3):
                for j in range(FEAT // 256):
                    rows = slice(m * HEAD, (m + 1) * HEAD)
                    cols = slice(j * 256, (j + 1) * 256)
                    total = qgown[rows, cols]
                    for off in range(3):
                        total += qgin[off, rows, cols].astype(f32)
                    out[m, j * 256 : (j + 1) * 256, :] = total.T
            local(out, qg_h, lsem.at[18]).wait()

        pl.run_scoped(sum_q, pltpu.VMEM((3, FEAT, HEAD), f32))
        wait_bytes(og8in, rsem.at[E8])

        def sum_o(out):
            def put_out(cols, x):
                total = x
                for off in range(3):
                    total += og8in[off, :, cols].astype(f32)
                out[:, cols] = total

            og_share(w, put_out)
            local(out, og_h, lsem.at[19]).wait()

        pl.run_scoped(sum_o, pltpu.VMEM((HEAD, FEAT), f32))
        gg_copy.wait()

        wait_bytes(wcx.at[pl.ds(0, (NB - 1) * HEAD), :], ssem.at[EW])
        wait_bytes(wtx.at[pl.ds(0, (NB - 1) * HEAD), :], ssem.at[ET])
        wait_bytes(gen_rows, ssem.at[EG])
        wait_bytes(ac.at[:, pl.ds(0, (NB - 1) * HEAD)], ssem.at[EA])
        wait_bytes(ag.at[:, pl.ds(0, (NB - 1) * HEAD)], ssem.at[EU])
        wait_bytes(gain_in.at[pl.ds(0, NB - 1)], ssem.at[EB])
        wait_bytes(abs_in.at[pl.ds(0, NB - 1)], ssem.at[ES])
        wait_bytes(diff_in.at[:, pl.ds(0, 7 * COLS)], ssem.at[ED])
        wait_bytes(qgin, ssem.at[EQ])
        wait_bytes(og8in, ssem.at[E8])

    pl.run_scoped(
        later_phase,
        pltpu.VMEM((NB, ROWS, HEAD), bf16),
        pltpu.VMEM((NB, HEAD, COLS), bf16),
        pltpu.VMEM((ROWS, COLS), bf16),
        pltpu.VMEM((ROWS, COLS), f32),
        pltpu.VMEM((8, 128), f32),
        pltpu.VMEM((3, 3 * HEAD, FEAT), bf16),
        pltpu.VMEM((3 * HEAD, FEAT), f32),
        pltpu.VMEM((LEN, HEAD), bf16),
        pltpu.VMEM((HEAD, LEN), f32),
        pltpu.VMEM((HEAD, LEN), f32),
        pltpu.VMEM((LEN, 3 * HEAD), f32),
        pltpu.VMEM((3 * HEAD, LEN), bf16),
        pltpu.VMEM((3, HEAD, FEAT), bf16),
    )


def body(
    noisy, generated, caption, null_caption, caption_drop, timestep, window_start,
    teacher_qkv, teacher_out, teacher_gain, teacher_qk_gain,
    critic_qkv, critic_out, critic_gain, critic_qk_gain,
):
    fraction = (timestep.astype(f32) + 1.0) / 1001.0
    noise_level = 5.0 * fraction / (1.0 + 4.0 * fraction)
    used_caption = jnp.where(caption_drop[0] == 1, null_caption, caption[0])
    caps16 = jnp.zeros((PAD, D), bf16).at[0].set(used_caption).at[1].set(null_caption)
    caps = jnp.concatenate([caps16[0:8].astype(f32)], axis=0)
    cosine, sine = rope_tables(window_start[0])
    wc = (critic_qkv.astype(f32) * critic_gain[None, :, None]).astype(bf16)
    wt = (teacher_qkv.astype(f32) * teacher_gain[None, :, None]).astype(bf16)
    level = jnp.broadcast_to(noise_level[:, None], (8, 128))
    hbm = pl.BlockSpec(memory_space=pl.ANY)
    vmem = pl.BlockSpec(memory_space=pltpu.VMEM)
    gg, qg, og, unused = pl.pallas_call(
        step_kernel,
        name="generator_step",
        out_shape=(
            jax.ShapeDtypeStruct((128, D), bf16),
            jax.ShapeDtypeStruct((3, FEAT, HEAD), f32),
            jax.ShapeDtypeStruct((HEAD, FEAT), f32),
            jax.ShapeDtypeStruct((NB, HEAD, COLS), bf16),
        ),
        in_specs=[hbm] * 6 + [vmem] * 5 + [hbm] * 3,
        out_specs=(hbm, hbm, hbm, hbm),
        scratch_shapes=[
            pltpu.VMEM((NR, BLK, D), bf16),
            pltpu.VMEM((NB * HEAD, COLS), bf16),
            pltpu.VMEM((NB * HEAD, COLS), bf16),
            pltpu.VMEM((ROWS, NB * HEAD), bf16),
            pltpu.VMEM((ROWS, NB * HEAD), bf16),
            pltpu.VMEM((NB, ROWS, HEAD), bf16),
            pltpu.VMEM((3, 3 * HEAD, FEAT), bf16),
            pltpu.VMEM((3, HEAD, FEAT), bf16),
            pltpu.VMEM((128, D), bf16),
            pltpu.VMEM((NB, 8, 128), f32),
            pltpu.VMEM((ROWS, COLS), bf16),
            pltpu.VMEM((LEN, HEAD), f32),
            pltpu.VMEM((LEN, HEAD), f32),
            pltpu.VMEM((LEN, HEAD), f32),
            pltpu.VMEM((LEN, HEAD), f32),
            pltpu.VMEM((LEN, HEAD), bf16),
            pltpu.VMEM((LEN, HEAD), bf16),
            pltpu.VMEM((LEN, HEAD), bf16),
            pltpu.VMEM((NR, ROWS, HEAD), f32),
            pltpu.VMEM((NR, ROWS, HEAD), f32),
            pltpu.VMEM((LEN, HEAD), f32),
            pltpu.VMEM((LEN, HEAD), f32),
            pltpu.VMEM((LEN, HEAD), f32),
            pltpu.VMEM((LEN, HEAD), bf16),
            pltpu.VMEM((LEN, HEAD), bf16),
            pltpu.SemaphoreType.DMA((20,)),
            pltpu.SemaphoreType.DMA((11,)),
            pltpu.SemaphoreType.DMA((11,)),
        ],
        compiler_params=pltpu.CompilerParams(
            collective_id=0, has_side_effects=True, vmem_limit_bytes=64 * 1024 * 1024
        ),
    )(
        noisy[0], wc, wt, caps16, cosine, sine, critic_qk_gain, teacher_qk_gain, level, caps,
        critic_gain[None, :], generated[0], critic_out, teacher_out,
    )
    return (gg[None], qg, og)


def solution(mesh):
    in_specs = (
        P("rep", None, None),
        P("rep", "seq", None),
        P("rep", None),
        P(),
        P("rep"),
        P("rep"),
        P("rep"),
        P(None, None, ("branch", "seq")),
        P(("branch", "seq"), None),
        P(),
        P(None, ("branch", "seq")),
        P(None, None, ("branch", "seq")),
        P(("branch", "seq"), None),
        P(),
        P(None, ("branch", "seq")),
    )
    out_specs = (
        P("rep", "seq", None),
        P(None, "rep", ("branch", "seq")),
        P(("branch", "seq"), "rep"),
    )
    return jax.shard_map(body, mesh=mesh, in_specs=in_specs, out_specs=out_specs, check_vma=False)
```

```python
import jax
import jax.numpy as jnp
from jax import lax
from jax.experimental import pallas as pl
from jax.experimental.pallas import tpu as pltpu
from jax.sharding import PartitionSpec as P

LEN = 1024
GRID_H = 30
GRID_W = 52
D = 5120
HEAD = 128
NB = 32
ROWS = 256
COLS = 640
NR = LEN // ROWS
PAD = 16
BLK = ROWS + PAD
FEAT = 1280

guidance = 5.0
score_scale = 128.0 ** (-0.5)
norm_eps = 1e-06
f32 = jnp.float32
bf16 = jnp.bfloat16
MESH = pl.DeviceIdType.MESH


def rope_tables(first_token):
    token_index = first_token + jnp.arange(LEN, dtype=jnp.int32)
    plane_size = GRID_H * GRID_W
    frame_index = token_index // plane_size
    remainder = token_index - frame_index * plane_size
    row_index = remainder // GRID_W
    column_index = remainder - row_index * GRID_W
    pair_index = jnp.arange(64, dtype=jnp.int32)
    in_frames = pair_index < 22
    in_rows = jnp.logical_and(pair_index >= 22, pair_index < 43)
    local_rank = jnp.where(
        in_frames, pair_index, jnp.where(in_rows, pair_index - 22, pair_index - 43)
    ).astype(f32)
    axis_width = jnp.where(in_frames, 44.0, 42.0).astype(f32)
    frequency = jnp.exp(-jnp.log(10000.0) * 2.0 * local_rank / axis_width)
    chosen = jnp.where(
        in_frames[None, :],
        frame_index[:, None],
        jnp.where(in_rows[None, :], row_index[:, None], column_index[:, None]),
    ).astype(f32)
    angles = chosen * frequency[None, :]
    cosine = jnp.cos(angles)
    sine = jnp.sin(angles)
    return (
        jnp.concatenate([cosine, cosine], axis=1),
        jnp.concatenate([-sine, sine], axis=1),
    )


def dot(a, b):
    return jnp.dot(a, b, preferred_element_type=f32)


def dot_nt(a, b):
    return lax.dot_general(a, b, (((1,), (1,)), ((), ())), preferred_element_type=f32)


def dot_tn(a, b):
    return lax.dot_general(a, b, (((0,), (0,)), ((), ())), preferred_element_type=f32)


def half_turn(x):
    return pltpu.roll(x, 64, 1)


def step_kernel(
    noisy_h, wc_h, wt_h, caps_h, cos_h, sin_h, cqk, tqk, level, caps, cgain, gen_h, cout_h, tout_h,
    gg_h, qg_h, og_h,
    noisy, wcx, wtx, ac, ag, cotf, qgin, og8in, diff_in, abs_in, gen, cos, sin,
    qraw, kraw, qr, kr, vv, rc, rn, invq, invk, linv, fa, gt,
    lsem, rsem, ssem,
):
    b = lax.axis_index("branch")
    s = lax.axis_index("seq")
    w = lax.axis_index("rep")
    core = lax.rem(b, 2)
    z_hi = b // 2
    z_lo = s // 4
    x_at = lax.rem(s, 4)
    z_at = z_hi * 2 + z_lo
    me = b * 8 + s
    myc = z_hi * 4 + x_at
    myr = z_lo * 2 + core

    def plane(q):
        return {"branch": q // 8, "seq": lax.rem(q, 8)}

    def col_of(q):
        return (q // 16) * 4 + lax.rem(q, 4)

    def row_of(q):
        return (lax.rem(q, 8) // 4) * 2 + lax.rem(q // 8, 2)

    def tile_of(r, c):
        return (c // 4) * 16 + lax.rem(r, 2) * 8 + (r // 2) * 4 + lax.rem(c, 4)

    def peer(k):
        return lax.rem(me + k, NB)

    sibling = {"branch": b + 1 - 2 * core}

    def along_x(k):
        return {"seq": z_lo * 4 + lax.rem(x_at + k, 4)}

    def along_z(k):
        z = lax.rem(z_at + k, 4)
        return {"branch": (z // 2) * 2 + core, "seq": lax.rem(z, 2) * 4 + x_at}

    def window(k):
        return {"rep": lax.rem(w + k, 4)}

    WC1, WC2, WC3, WT1, WT2, WT3, EG, EA, EU, C1A, C1B, C2A, C2B, C3, ED, ES, EQ, E8 = range(18)

    def send(src, dst, e, device):
        pltpu.make_async_remote_copy(
            src_ref=src, dst_ref=dst, send_sem=ssem.at[e], recv_sem=rsem.at[e],
            device_id=device, device_id_type=MESH,
        ).start()

    def local(src, dst, sem):
        c = pltpu.make_async_copy(src, dst, sem)
        c.start()
        return c

    def local_in(src, dst, e):
        pltpu.make_async_copy(src, dst, rsem.at[e]).start()

    def wait_in(ref, e):
        pltpu.make_async_copy(ref, ref, rsem.at[e]).wait()

    def wait_out(ref, e):
        pltpu.make_async_copy(ref, ref, ssem.at[e]).wait()

    for i in range(NR):
        local(noisy_h.at[pl.ds(i * ROWS, ROWS), :], noisy.at[i, pl.ds(0, ROWS), :], lsem.at[i])
    cap_copies = [local(caps_h, noisy.at[i, pl.ds(ROWS, PAD), :], lsem.at[4 + i]) for i in range(NR)]
    cos_copy = local(cos_h, cos, lsem.at[8])
    sin_copy = local(sin_h, sin, lsem.at[9])

    barrier = pltpu.get_barrier_semaphore()

    @pl.loop(1, NB)
    def _(k):
        pl.semaphore_signal(barrier, inc=1, device_id=plane(peer(k)), device_id_type=MESH)

    for k in range(1, 4):
        pl.semaphore_signal(barrier, inc=1, device_id=window(k), device_id_type=MESH)
    pl.semaphore_wait(barrier, NB - 1 + 3)

    quarter = pl.ds(pl.multiple_of(w * 32, 32), 32)
    runs = [pl.ds(pl.multiple_of(z * 16 + core * 8, 8), 8) for z in range(2)]

    def weights_1(src, dst, e):
        mine = dst.at[me, quarter, :]

        @pl.loop(1, 16)
        def _(k):
            t = lax.rem(z_hi * 8 + s + k, 16)
            q = (t // 8) * 16 + core * 8 + lax.rem(t, 8)
            cols = pl.ds(pl.multiple_of(col_of(q) * COLS, COLS), COLS)
            send(src.at[quarter, cols], mine, e, plane(q))

        local_in(src.at[quarter, pl.ds(pl.multiple_of(myc * COLS, COLS), COLS)], mine, e)

    def weights_2(dst, e):
        wait_in(dst.at[pl.ds(0, 16), pl.ds(0, 32), :], e - 1)
        for k in (2, 1, 3):
            for run in runs:
                send(dst.at[run, quarter, :], dst.at[run, quarter, :], e, window(k))

    def weights_3(dst, e):
        wait_in(dst.at[pl.ds(0, 16), pl.ds(0, 96), :], e - 1)
        for run in runs:
            send(dst.at[run], dst.at[run], e, sibling)

    weights_1(cout_h, wcx, WC1)
    weights_1(tout_h, wtx, WT1)

    gen_rows = gen.at[pl.ds(pl.multiple_of(lax.rem(s, 2) * 128, 128), 128), :]
    has_rows = x_at // 2 == core

    @pl.when(has_rows)
    def _():
        @pl.loop(1, 4)
        def _(k):
            c = z_hi * 4 + lax.rem(x_at + k, 4)
            cols = pl.ds(pl.multiple_of(c * COLS, COLS), COLS)
            send(gen_h.at[:, cols], gen_rows, EG, along_x(k))

        local_in(gen_h.at[:, pl.ds(pl.multiple_of(myc * COLS, COLS), COLS)], gen_rows, EG)

    def tokens(src, dst, e):
        mine = dst.at[:, pl.ds(pl.multiple_of(me * HEAD, HEAD), HEAD)]

        @pl.loop(1, NB)
        def _(k):
            q = peer(k)
            send(src.at[pl.ds(pl.multiple_of(row_of(q) * ROWS, ROWS), ROWS), :], mine, e, plane(q))

        local_in(src.at[pl.ds(pl.multiple_of(myr * ROWS, ROWS), ROWS), :], mine, e)

    def forward_phase(wall, pbuf, att_a, tq, tk, tv):
        def load_w(j):
            src = wc_h if j < 3 else wt_h
            return local(src.at[j % 3], wall.at[:, pl.ds(j * HEAD, HEAD)], lsem.at[10 + j])

        w_copies = [load_w(j) for j in range(6)]

        for c in cap_copies:
            c.wait()
        for c in w_copies[:4]:
            c.wait()

        @pl.loop(0, NR)
        def _(i):
            pltpu.make_async_copy(
                noisy_h.at[pl.ds(i * ROWS, ROWS), :], noisy.at[i, pl.ds(0, ROWS), :], lsem.at[i]
            ).wait()
            pbuf[i, :, 0:512] = dot(noisy[i], wall[:, 0:512])
            for half in range(2):
                top = half * 128
                acc_c = jnp.zeros((128, 128), f32)
                acc_n = jnp.zeros((128, 128), f32)
                for j in range(D // 128):
                    x = noisy[i, top : top + 128, j * 128 : j * 128 + 128].astype(f32)
                    u = x + caps[0:1, j * 128 : j * 128 + 128]
                    v = x + caps[1:2, j * 128 : j * 128 + 128]
                    acc_c += u * u
                    acc_n += v * v
                sum_c = jnp.sum(acc_c, axis=1, keepdims=True) * (1.0 / D)
                sum_n = jnp.sum(acc_n, axis=1, keepdims=True) * (1.0 / D)
                rc[i, top : top + 128, :] = jnp.broadcast_to(
                    lax.rsqrt(sum_c + norm_eps), (128, 128)
                )
                rn[i, top : top + 128, :] = jnp.broadcast_to(
                    lax.rsqrt(sum_n + norm_eps), (128, 128)
                )

        weights_2(wcx, WC2)
        cos_copy.wait()
        sin_copy.wait()

        def attention(col, row, scale_ref, gains, tables, keep, out):
            q_ref, k_ref, v_ref = tables

            @pl.loop(0, NR)
            def _(i):
                rows = pl.ds(pl.multiple_of(i * ROWS, ROWS), ROWS)
                scale = scale_ref[i]
                cosine = cos[rows, :]
                sine = sin[rows, :]

                def raw(m):
                    block = pbuf[i, 0:ROWS, col + m * HEAD : col + (m + 1) * HEAD]
                    shift = pbuf[
                        i, ROWS + row : ROWS + row + 1, col + m * HEAD : col + (m + 1) * HEAD
                    ]
                    return scale * (block + shift)

                for m, (dst, raw_ref, inv_ref) in enumerate(
                    ((q_ref, qraw, invq), (k_ref, kraw, invk))
                ):
                    x = raw(m)
                    inverse = lax.rsqrt(jnp.mean(x * x, axis=1, keepdims=True) + norm_eps)
                    normed = x * inverse * gains[m : m + 1, :]
                    dst[rows, :] = (normed * cosine + half_turn(normed) * sine).astype(bf16)
                    if keep:
                        raw_ref[rows, :] = x
                        inv_ref[rows, :] = jnp.broadcast_to(inverse, (ROWS, HEAD))
                v_ref[rows, :] = raw(2).astype(bf16)

            @pl.loop(0, NR)
            def _(i):
                rows = pl.ds(pl.multiple_of(i * ROWS, ROWS), ROWS)
                exponent = jnp.exp(dot_nt(q_ref[rows, :], k_ref[...]) * score_scale)
                inverse = 1.0 / jnp.sum(exponent, axis=1, keepdims=True)
                if keep:
                    linv[rows, :] = jnp.broadcast_to(inverse, (ROWS, HEAD))
                prob = (exponent * inverse).astype(bf16)
                out(rows, dot(prob, v_ref[...]).astype(bf16))

        def to_a(rows, x):
            att_a[rows, :] = x

        def to_fake(rows, x):
            fa[rows, :] = x

        def to_guided(rows, x):
            gt[rows, :] = (
                guidance * att_a[rows, :].astype(f32) - (guidance - 1.0) * x.astype(f32)
            ).astype(bf16)

        attention(0, 0, rc, cqk, (qr, kr, vv), True, to_fake)
        tokens(fa, ac, EA)
        weights_2(wtx, WT2)
        for c in w_copies[4:]:
            c.wait()

        @pl.loop(0, NR)
        def _(i):
            pbuf[i, :, 512:768] = dot(noisy[i], wall[:, 512:768])

        attention(384, 0, rc, tqk, (tq, tk, tv), False, to_a)
        attention(384, 1, rn, tqk, (tq, tk, tv), False, to_guided)
        tokens(gt, ag, EU)

    pl.run_scoped(
        forward_phase,
        pltpu.VMEM((D, 6 * HEAD), bf16),
        pltpu.VMEM((NR, BLK, 6 * HEAD), f32),
        pltpu.VMEM((LEN, HEAD), bf16),
        pltpu.VMEM((LEN, HEAD), bf16),
        pltpu.VMEM((LEN, HEAD), bf16),
        pltpu.VMEM((LEN, HEAD), bf16),
    )

    noise = level[0:1, 0:1]

    def later_phase(cout, diff_out, fake, abs_out, qgout, qgown, gk, gv, rgt, og8, ogown):
        cout_copy = local(cout_h, cout, lsem.at[16])
        tile_cols = pl.ds(pl.multiple_of(myc * COLS, COLS), COLS)
        weights_3(wcx, WC3)
        wait_in(gen, EG)
        wait_in(ac, EA)
        wait_in(wcx.at[pl.ds(0, 16)], WC3)

        def predictions(i, total, guided):
            rows = pl.ds(pl.multiple_of(i * 128, 128), 128)
            latent = noisy[myr, rows, tile_cols].astype(f32)
            cond = latent + caps[0:1, tile_cols]
            if guided:
                null = latent + caps[1:2, tile_cols]
                velocity = guidance * cond - (guidance - 1.0) * null + total
            else:
                velocity = cond + total
            return latent - noise * velocity

        def product(att, weights, rows):
            return dot(att[rows, :], weights[...].reshape(NB * HEAD, COLS))

        def cotangent(i):
            rows = pl.ds(i * 128, 128)
            fake_pred = predictions(i, product(ac, wcx, rows), False)
            target = gen[rows, :].astype(f32)
            cotf[me, rows, :] = (-noise * (fake_pred - target) * (1.0 / 64.0)).astype(bf16)
            fake[rows, :] = fake_pred

        top, low = pl.ds(0, 128), pl.ds(128, 128)
        cotangent(0)
        for k in (2, 1, 3):
            send(cotf.at[me, top, :], cotf.at[me, top, :], C1A, along_x(k))
        cotangent(1)
        for k in (2, 1, 3):
            send(cotf.at[me, low, :], cotf.at[me, low, :], C1B, along_z(k))
        wait_in(cotf.at[pl.ds(0, 3), top, :], C1A)
        x_run = pl.ds(me - x_at, 4)
        for k in (2, 1, 3):
            send(cotf.at[x_run, top, :], cotf.at[x_run, top, :], C2A, along_z(k))
        wait_in(cotf.at[pl.ds(0, 3), low, :], C1B)
        for k in (2, 1, 3):
            for z in range(4):
                held = cotf.at[(z // 2) * 16 + core * 8 + (z % 2) * 4 + x_at, low, :]
                send(held, held, C2B, along_x(k))
        cout_copy.wait()
        wait_in(cotf.at[pl.ds(0, 12), top, :], C2A)
        wait_in(cotf.at[pl.ds(0, 12), low, :], C2B)
        for run in runs:
            send(cotf.at[run], cotf.at[run], C3, sibling)

        gk[...] = jnp.zeros_like(gk)
        gv[...] = jnp.zeros_like(gv)

        def undo(rows, raw_ref, inv_ref, gain, grad):
            turned = grad * cos[rows, :] + half_turn(grad * sin[rows, :])
            scaled = gain * turned
            raw = raw_ref[rows, :]
            inverse = inv_ref[rows, :]
            back = inverse * scaled - raw * inverse * inverse * inverse * jnp.mean(
                scaled * raw, axis=1, keepdims=True
            )
            return back.astype(bf16).astype(f32)

        def backward_rows(side):
            @pl.loop(0, 2)
            def _(j):
                i = j * 2 + side
                rows = pl.ds(pl.multiple_of(i * ROWS, ROWS), ROWS)
                total = jnp.zeros((ROWS, HEAD), f32)
                for c in range(8):
                    total += dot_nt(cotf[tile_of(i, c)], cout[:, c * COLS : (c + 1) * COLS])
                grads = total.astype(bf16)
                inverse = linv[rows, :][:, 0:1]
                prob = jnp.exp(dot_nt(qr[rows, :], kr[...]) * score_scale) * inverse
                grad_prob = dot_nt(grads, vv[...])
                mean = jnp.sum(grad_prob * prob, axis=1, keepdims=True)
                grad_score = (prob * (grad_prob - mean) * score_scale).astype(bf16)
                gq = dot(grad_score, kr[...])
                gk[...] += dot_tn(qr[rows, :], grad_score)
                gv[...] += dot_tn(grads, prob.astype(bf16))
                rg = rc[i] * undo(rows, qraw, invq, cqk[0:1, :], gq)
                rgt[0:HEAD, rows] = rg.T.astype(bf16)

        backward_rows(core)
        wait_in(cotf.at[pl.ds(0, 16)], C3)

        def og_share(target, put):
            for half in range(2):
                total = jnp.zeros((HEAD, COLS), f32)
                for r in range(NR):
                    total += dot_tn(
                        fa[r * ROWS : (r + 1) * ROWS, :], cotf[tile_of(r, target * 2 + half)]
                    )
                put(pl.ds(half * COLS, COLS), total)

        @pl.loop(0, 3)
        def _(n):
            off = lax.rem(n + 1, 3) + 1
            target = lax.rem(w + off, 4)

            def put8(cols, x):
                og8[off - 1, :, cols] = x.astype(bf16)

            og_share(target, put8)
            send(og8.at[off - 1], og8in.at[off - 1], E8, {"rep": target})

        backward_rows(1 - core)

        for i in range(NR):
            rows = pl.ds(i * ROWS, ROWS)
            grad_k = gk[:, i * ROWS : (i + 1) * ROWS].T
            grad_v = gv[:, i * ROWS : (i + 1) * ROWS].T
            grad_k = rc[i] * undo(rows, kraw, invk, cqk[1:2, :], grad_k)
            grad_v = rc[i] * grad_v.astype(bf16).astype(f32)
            rgt[HEAD : 2 * HEAD, rows] = grad_k.T.astype(bf16)
            rgt[2 * HEAD :, rows] = grad_v.T.astype(bf16)
        row_sum = jnp.sum(rgt[...].astype(f32), axis=1, keepdims=True)

        def share(target, put):
            @pl.loop(0, FEAT // 256)
            def _(j):
                cols = pl.ds(pl.multiple_of(target * FEAT + j * 256, 256), 256)
                total = row_sum * caps[0:1, cols]
                for i in range(NR):
                    total += dot(rgt[:, i * ROWS : (i + 1) * ROWS], noisy[i, 0:ROWS, cols])
                put(pl.ds(pl.multiple_of(j * 256, 256), 256), total * cgain[0:1, cols])

        for off in (2, 1, 3):
            target = lax.rem(w + off, 4)

            def put(cols, x, off=off):
                qgout[off - 1, :, cols] = x.astype(bf16)

            share(target, put)
            send(qgout.at[off - 1], qgin.at[off - 1], EQ, {"rep": target})

        def put_own(cols, x):
            qgown[:, cols] = x

        share(w, put_own)

        weights_3(wtx, WT3)
        wait_in(ag, EU)
        wait_in(wtx.at[pl.ds(0, 16)], WT3)
        abs_out[...] = jnp.zeros_like(abs_out)

        @pl.loop(0, 2)
        def _(i):
            rows = pl.ds(pl.multiple_of(i * 128, 128), 128)
            real_pred = predictions(i, product(ag, wtx, rows), True)
            target = gen[rows, :].astype(f32)
            gap = jnp.abs(real_pred - target)
            lanes = gap[:, 0:128]
            for j in range(1, COLS // 128):
                lanes += gap[:, j * 128 : (j + 1) * 128]
            eight = lanes[0:8, :]
            for j in range(1, 16):
                eight += lanes[j * 8 : (j + 1) * 8, :]
            abs_out[...] += eight
            diff_out[rows, :] = (fake[rows, :] - real_pred).astype(bf16)

        @pl.loop(1, NB)
        def _(k):
            send(abs_out, abs_in.at[me], ES, plane(peer(k)))

        local_in(abs_out, abs_in.at[me], ES)

        diff_mine = diff_in.at[:, tile_cols]

        @pl.loop(0, 8)
        def _(t):
            e = lax.rem(t, 2)
            to_b = t // 2
            to_s = myr * 2 + e
            src = diff_out.at[pl.ds(pl.multiple_of(e * 128, 128), 128), :]
            mine = to_b * 8 + to_s == me

            @pl.when(mine)
            def _():
                local_in(src, diff_mine, ED)

            @pl.when(jnp.logical_not(mine))
            def _():
                send(src, diff_mine, ED, {"branch": to_b, "seq": to_s})

        og_share(w, lambda cols, x: ogown.__setitem__((slice(None), cols), x))

        wait_in(abs_in, ES)
        wait_in(diff_in, ED)
        spread = jnp.sum(jnp.sum(abs_in[...], axis=0), axis=(0, 1), keepdims=True) * (
            1.0 / (LEN * D)
        )
        factor = 1.0 / (spread + 1e-05)

        @pl.loop(0, 8)
        def _(j):
            cols = pl.ds(pl.multiple_of(j * COLS, COLS), COLS)
            diff_in[:, cols] = (diff_in[:, cols].astype(f32) * factor).astype(bf16)

        gg_copy = local(diff_in, gg_h, lsem.at[17])

        wait_in(og8in, E8)
        for j in range(5):
            cols = slice(j * 256, (j + 1) * 256)
            total = ogown[:, cols]
            for off in range(3):
                total += og8in[off, :, cols].astype(f32)
            ogown[:, cols] = total
        og_copy = local(ogown, og_h, lsem.at[19])
        wait_in(qgin, EQ)

        def sum_q(out):
            for m in range(3):
                for j in range(FEAT // 256):
                    rows = slice(m * HEAD, (m + 1) * HEAD)
                    cols = slice(j * 256, (j + 1) * 256)
                    total = qgown[rows, cols]
                    for off in range(3):
                        total += qgin[off, rows, cols].astype(f32)
                    out[m, j * 256 : (j + 1) * 256, :] = total.T
            local(out, qg_h, lsem.at[18]).wait()

        pl.run_scoped(sum_q, pltpu.VMEM((3, FEAT, HEAD), f32))
        og_copy.wait()
        gg_copy.wait()

        for dst, e in ((wcx, WC1), (wtx, WT1)):
            wait_out(dst.at[pl.ds(0, 15), pl.ds(0, 32), :], e)
            wait_out(dst.at[pl.ds(0, 16), pl.ds(0, 96), :], e + 1)
            wait_out(dst.at[pl.ds(0, 16)], e + 2)

        @pl.when(has_rows)
        def _():
            wait_out(diff_in.at[:, pl.ds(0, 3 * COLS)], EG)

        wait_out(ac.at[:, pl.ds(0, (NB - 1) * HEAD)], EA)
        wait_out(ag.at[:, pl.ds(0, (NB - 1) * HEAD)], EU)
        wait_out(cotf.at[pl.ds(0, 3), top, :], C1A)
        wait_out(cotf.at[pl.ds(0, 3), low, :], C1B)
        wait_out(cotf.at[pl.ds(0, 12), top, :], C2A)
        wait_out(cotf.at[pl.ds(0, 12), low, :], C2B)
        wait_out(cotf.at[pl.ds(0, 16)], C3)
        wait_out(abs_in.at[pl.ds(0, NB - 1)], ES)

        @pl.when(has_rows)
        def _():
            wait_out(diff_in.at[:, pl.ds(0, 7 * COLS)], ED)

        @pl.when(jnp.logical_not(has_rows))
        def _():
            wait_out(diff_in, ED)

        wait_out(qgin, EQ)
        wait_out(og8in, E8)

    pl.run_scoped(
        later_phase,
        pltpu.VMEM((HEAD, D), bf16),
        pltpu.VMEM((ROWS, COLS), bf16),
        pltpu.VMEM((ROWS, COLS), f32),
        pltpu.VMEM((8, 128), f32),
        pltpu.VMEM((3, 3 * HEAD, FEAT), bf16),
        pltpu.VMEM((3 * HEAD, FEAT), f32),
        pltpu.VMEM((HEAD, LEN), f32),
        pltpu.VMEM((HEAD, LEN), f32),
        pltpu.VMEM((3 * HEAD, LEN), bf16),
        pltpu.VMEM((3, HEAD, FEAT), bf16),
        pltpu.VMEM((HEAD, FEAT), f32),
    )


def body(
    noisy, generated, caption, null_caption, caption_drop, timestep, window_start,
    teacher_qkv, teacher_out, teacher_gain, teacher_qk_gain,
    critic_qkv, critic_out, critic_gain, critic_qk_gain,
):
    fraction = (timestep.astype(f32) + 1.0) / 1001.0
    noise_level = 5.0 * fraction / (1.0 + 4.0 * fraction)
    used_caption = jnp.where(caption_drop[0] == 1, null_caption, caption[0])
    caps16 = jnp.zeros((PAD, D), bf16).at[0].set(used_caption).at[1].set(null_caption)
    caps = jnp.concatenate([caps16[0:8].astype(f32)], axis=0)
    cosine, sine = rope_tables(window_start[0])
    wc = (critic_qkv.astype(f32) * critic_gain[None, :, None]).astype(bf16)
    wt = (teacher_qkv.astype(f32) * teacher_gain[None, :, None]).astype(bf16)
    level = jnp.broadcast_to(noise_level[:, None], (8, 128))
    hbm = pl.BlockSpec(memory_space=pl.ANY)
    vmem = pl.BlockSpec(memory_space=pltpu.VMEM)
    gg, qg, og = pl.pallas_call(
        step_kernel,
        name="generator_step",
        out_shape=(
            jax.ShapeDtypeStruct((128, D), bf16),
            jax.ShapeDtypeStruct((3, FEAT, HEAD), f32),
            jax.ShapeDtypeStruct((HEAD, FEAT), f32),
        ),
        in_specs=[hbm] * 6 + [vmem] * 5 + [hbm] * 3,
        out_specs=(hbm, hbm, hbm),
        scratch_shapes=[
            pltpu.VMEM((NR, BLK, D), bf16),
            pltpu.VMEM((NB, HEAD, COLS), bf16),
            pltpu.VMEM((NB, HEAD, COLS), bf16),
            pltpu.VMEM((ROWS, NB * HEAD), bf16),
            pltpu.VMEM((ROWS, NB * HEAD), bf16),
            pltpu.VMEM((NB, ROWS, COLS), bf16),
            pltpu.VMEM((3, 3 * HEAD, FEAT), bf16),
            pltpu.VMEM((3, HEAD, FEAT), bf16),
            pltpu.VMEM((128, D), bf16),
            pltpu.VMEM((NB, 8, 128), f32),
            pltpu.VMEM((ROWS, COLS), bf16),
            pltpu.VMEM((LEN, HEAD), f32),
            pltpu.VMEM((LEN, HEAD), f32),
            pltpu.VMEM((LEN, HEAD), f32),
            pltpu.VMEM((LEN, HEAD), f32),
            pltpu.VMEM((LEN, HEAD), bf16),
            pltpu.VMEM((LEN, HEAD), bf16),
            pltpu.VMEM((LEN, HEAD), bf16),
            pltpu.VMEM((NR, ROWS, HEAD), f32),
            pltpu.VMEM((NR, ROWS, HEAD), f32),
            pltpu.VMEM((LEN, HEAD), f32),
            pltpu.VMEM((LEN, HEAD), f32),
            pltpu.VMEM((LEN, HEAD), f32),
            pltpu.VMEM((LEN, HEAD), bf16),
            pltpu.VMEM((LEN, HEAD), bf16),
            pltpu.SemaphoreType.DMA((20,)),
            pltpu.SemaphoreType.DMA((18,)),
            pltpu.SemaphoreType.DMA((18,)),
        ],
        compiler_params=pltpu.CompilerParams(
            collective_id=0, has_side_effects=True, vmem_limit_bytes=64 * 1024 * 1024
        ),
    )(
        noisy[0], wc, wt, caps16, cosine, sine, critic_qk_gain, teacher_qk_gain, level, caps,
        critic_gain[None, :], generated[0], critic_out, teacher_out,
    )
    return (gg[None], qg, og)


def solution(mesh):
    in_specs = (
        P("rep", None, None),
        P("rep", "seq", None),
        P("rep", None),
        P(),
        P("rep"),
        P("rep"),
        P("rep"),
        P(None, None, ("branch", "seq")),
        P(("branch", "seq"), None),
        P(),
        P(None, ("branch", "seq")),
        P(None, None, ("branch", "seq")),
        P(("branch", "seq"), None),
        P(),
        P(None, ("branch", "seq")),
    )
    out_specs = (
        P("rep", "seq", None),
        P(None, "rep", ("branch", "seq")),
        P(("branch", "seq"), "rep"),
    )
    return jax.shard_map(body, mesh=mesh, in_specs=in_specs, out_specs=out_specs, check_vma=False)
```

```python
import jax
import jax.numpy as jnp
from jax import lax
from jax.experimental import pallas as pl
from jax.experimental.pallas import tpu as pltpu
from jax.sharding import PartitionSpec as P

LEN = 1024
GRID_H = 30
GRID_W = 52
D = 5120
HEAD = 128
NB = 32
ROWS = 256
COLS = 640
NR = LEN // ROWS
PAD = 16
BLK = ROWS + PAD
FEAT = 1280

guidance = 5.0
score_scale = 128.0 ** (-0.5)
norm_eps = 1e-06
f32 = jnp.float32
bf16 = jnp.bfloat16
MESH = pl.DeviceIdType.MESH


def rope_table():
    spot = jnp.arange(128, dtype=jnp.int32)[:, None]
    pair = jnp.arange(64, dtype=jnp.int32)[None, :]
    axis = jnp.where(pair < 22, 0, jnp.where(pair < 43, 1, 2))
    first = jnp.where(axis == 0, 0, jnp.where(axis == 1, 22, 43))
    width = jnp.where(axis == 0, 44.0, 42.0).astype(f32)
    frequency = jnp.exp(-jnp.log(10000.0) * 2.0 * (pair - first).astype(f32) / width)
    held = jnp.where(spot < 32, 0, jnp.where(spot < 64, 1, 2))
    place = spot - jnp.where(held == 0, 0, jnp.where(held == 1, 32, 64))
    angle = place.astype(f32) * frequency
    inside = held == axis
    cosine = jnp.where(inside, jnp.cos(angle), 0.0)
    sine = jnp.where(inside, jnp.sin(angle), 0.0)
    return jnp.concatenate([cosine, cosine, -sine, sine], axis=1)


def dot(a, b):
    return jnp.dot(a, b, preferred_element_type=f32)


def dot_nt(a, b):
    return lax.dot_general(a, b, (((1,), (1,)), ((), ())), preferred_element_type=f32)


def dot_tn(a, b):
    return lax.dot_general(a, b, (((0,), (0,)), ((), ())), preferred_element_type=f32)


def half_turn(x):
    return pltpu.roll(x, 64, 1)


def step_kernel(
    scalars, noisy_h, wc_h, wt_h, caption, null_caption, table, cqk, tqk, cgain, tgain,
    gen_h, cout_h, tout_h,
    gg_h, qg_h, og_h,
    noisy, wcx, wtx, ac, ag, gain_in, cotf, pair, ogsib, qgin, qgfwd, og8in, diff_in, abs_in, gen,
    cos, sin, caps, qraw, kraw, qr, kr, vv, rc, rn, invq, invk, linv, fa, gt,
    lsem, rsem, ssem,
):
    b = lax.axis_index("branch")
    s = lax.axis_index("seq")
    w = lax.axis_index("rep")
    core = lax.rem(b, 2)
    z_hi = b // 2
    z_lo = s // 4
    x_at = lax.rem(s, 4)
    z_at = z_hi * 2 + z_lo
    me = b * 8 + s
    myc = z_hi * 4 + x_at
    myr = z_lo * 2 + core

    def plane(q):
        return {"branch": q // 8, "seq": lax.rem(q, 8)}

    def col_of(q):
        return (q // 16) * 4 + lax.rem(q, 4)

    def row_of(q):
        return (lax.rem(q, 8) // 4) * 2 + lax.rem(q // 8, 2)

    def tile_of(r, c):
        return (c // 4) * 16 + lax.rem(r, 2) * 8 + (r // 2) * 4 + lax.rem(c, 4)

    def peer(k):
        return lax.rem(me + k, NB)

    sibling = {"branch": b + 1 - 2 * core}

    def along_x(k):
        return {"seq": z_lo * 4 + lax.rem(x_at + k, 4)}

    def along_z(k):
        z = lax.rem(z_at + k, 4)
        return {"branch": (z // 2) * 2 + core, "seq": lax.rem(z, 2) * 4 + x_at}

    def window(k):
        return {"rep": lax.rem(w + k, 4)}

    (
        WC1, WC2, WC3, WT1, WT2, WT3, EG, EA, EU, EB, C1A, C1B, C2A, C2B, FX, CS,
        ED, ES, QF0, QF1, QD0, QD1, QC0, QC1, E8,
    ) = range(25)

    def send(src, dst, e, device):
        pltpu.make_async_remote_copy(
            src_ref=src, dst_ref=dst, send_sem=ssem.at[e], recv_sem=rsem.at[e],
            device_id=device, device_id_type=MESH,
        ).start()

    def local(src, dst, sem):
        c = pltpu.make_async_copy(src, dst, sem)
        c.start()
        return c

    def local_in(src, dst, e):
        pltpu.make_async_copy(src, dst, rsem.at[e]).start()

    def wait_in(ref, e):
        pltpu.make_async_copy(ref, ref, rsem.at[e]).wait()

    def wait_out(ref, e):
        pltpu.make_async_copy(ref, ref, ssem.at[e]).wait()

    for i in range(NR):
        local(noisy_h.at[pl.ds(i * ROWS, ROWS), :], noisy.at[i, pl.ds(0, ROWS), :], lsem.at[i])

    barrier = pltpu.get_barrier_semaphore()

    @pl.loop(1, NB)
    def _(k):
        pl.semaphore_signal(barrier, inc=1, device_id=plane(peer(k)), device_id_type=MESH)

    for k in range(1, 4):
        pl.semaphore_signal(barrier, inc=1, device_id=window(k), device_id_type=MESH)
    pl.semaphore_wait(barrier, NB - 1 + 3)

    quarter = pl.ds(pl.multiple_of(w * 32, 32), 32)
    runs = [pl.ds(pl.multiple_of(z * 16 + core * 8, 8), 8) for z in range(2)]

    def weights_1(src, dst, e):
        mine = dst.at[me, quarter, :]

        @pl.loop(1, 16)
        def _(k):
            t = lax.rem(z_hi * 8 + s + k, 16)
            q = (t // 8) * 16 + core * 8 + lax.rem(t, 8)
            cols = pl.ds(pl.multiple_of(col_of(q) * COLS, COLS), COLS)
            send(src.at[quarter, cols], mine, e, plane(q))

        local_in(src.at[quarter, pl.ds(pl.multiple_of(myc * COLS, COLS), COLS)], mine, e)

    def weights_2(dst, e):
        wait_in(dst.at[pl.ds(0, 16), pl.ds(0, 32), :], e - 1)
        for k in (2, 1, 3):
            for run in runs:
                send(dst.at[run, quarter, :], dst.at[run, quarter, :], e, window(k))

    def weights_3(dst, e):
        wait_in(dst.at[pl.ds(0, 16), pl.ds(0, 96), :], e - 1)
        for run in runs:
            send(dst.at[run], dst.at[run], e, sibling)

    weights_1(cout_h, wcx, WC1)
    weights_1(tout_h, wtx, WT1)

    gen_rows = gen.at[pl.ds(pl.multiple_of(lax.rem(s, 2) * 128, 128), 128), :]
    has_rows = x_at // 2 == core

    @pl.when(has_rows)
    def _():
        @pl.loop(1, 4)
        def _(k):
            c = z_hi * 4 + lax.rem(x_at + k, 4)
            cols = pl.ds(pl.multiple_of(c * COLS, COLS), COLS)
            send(gen_h.at[:, cols], gen_rows, EG, along_x(k))

        local_in(gen_h.at[:, pl.ds(pl.multiple_of(myc * COLS, COLS), COLS)], gen_rows, EG)

    def tokens(src, dst, e):
        mine = dst.at[:, pl.ds(pl.multiple_of(me * HEAD, HEAD), HEAD)]

        @pl.loop(1, NB)
        def _(k):
            q = peer(k)
            send(src.at[pl.ds(pl.multiple_of(row_of(q) * ROWS, ROWS), ROWS), :], mine, e, plane(q))

        local_in(src.at[pl.ds(pl.multiple_of(myr * ROWS, ROWS), ROWS), :], mine, e)

    def forward_phase(wall, pbuf, tq, tk, tv):
        def load_w(j):
            src = wc_h if j < 3 else wt_h
            return local(src.at[j % 3], wall.at[:, pl.ds(j * HEAD, HEAD)], lsem.at[10 + j])

        w_copies = [load_w(j) for j in range(6)]

        dropped = jnp.full((40, 128), scalars[0, 0], jnp.int32) == 1
        null = null_caption[...]
        used = jnp.where(dropped, null, caption[...])
        caps[...] = jnp.zeros_like(caps)
        for j in range(40):
            caps[0:1, j * 128 : (j + 1) * 128] = used[j : j + 1, :]
            caps[1:2, j * 128 : (j + 1) * 128] = null[j : j + 1, :]
        below = jnp.concatenate([caps[...], jnp.zeros((8, D), f32)], axis=0).astype(bf16)
        for i in range(NR):
            noisy[i, ROWS:BLK, :] = below

        @pl.loop(0, NR)
        def _(i):
            token = (
                lax.broadcasted_iota(jnp.int32, (ROWS, 128), 0) + (scalars[0, 2] + i * ROWS)
            ).astype(f32)
            frame = jnp.floor((token + 0.5) * (1.0 / (GRID_H * GRID_W)))
            rest = token - frame * (GRID_H * GRID_W)
            row = jnp.floor((rest + 0.5) * (1.0 / GRID_W))
            column = rest - row * GRID_W
            lane = lax.broadcasted_iota(jnp.int32, (ROWS, 128), 1).astype(f32)
            place = jnp.where(
                lane < 32.0, frame, jnp.where(lane < 64.0, row + 32.0, column + 64.0)
            )
            both = jnp.dot(
                jnp.where(lane == place, 1.0, 0.0), table[...],
                preferred_element_type=f32, precision=lax.Precision.HIGHEST,
            )
            rows = pl.ds(pl.multiple_of(i * ROWS, ROWS), ROWS)
            cos[rows, :] = both[:, 0:128]
            sin[rows, :] = both[:, 128:256]

        def scale_w(gain, lo, hi):
            @pl.loop(0, 5)
            def _(t):
                columns = gain[pl.ds(pl.multiple_of(t * 8, 8), 8), :].T
                for n in range(8):
                    rows = pl.ds(pl.multiple_of(t * 1024 + n * 128, 128), 128)
                    wall[rows, lo:hi] = (
                        wall[rows, lo:hi].astype(f32) * columns[:, n : n + 1]
                    ).astype(bf16)

        for c in w_copies[:4]:
            c.wait()
        scale_w(cgain, 0, 384)
        scale_w(tgain, 384, 512)

        @pl.loop(0, NR)
        def _(i):
            pltpu.make_async_copy(
                noisy_h.at[pl.ds(i * ROWS, ROWS), :], noisy.at[i, pl.ds(0, ROWS), :], lsem.at[i]
            ).wait()
            pbuf[i, :, 0:512] = dot(noisy[i], wall[:, 0:512])
            for half in range(2):
                top = half * 128
                acc_c = jnp.zeros((128, 128), f32)
                acc_n = jnp.zeros((128, 128), f32)
                for j in range(D // 128):
                    x = noisy[i, top : top + 128, j * 128 : j * 128 + 128].astype(f32)
                    u = x + caps[0:1, j * 128 : j * 128 + 128]
                    v = x + caps[1:2, j * 128 : j * 128 + 128]
                    acc_c += u * u
                    acc_n += v * v
                sum_c = jnp.sum(acc_c, axis=1, keepdims=True) * (1.0 / D)
                sum_n = jnp.sum(acc_n, axis=1, keepdims=True) * (1.0 / D)
                rc[i, top : top + 128, :] = jnp.broadcast_to(
                    lax.rsqrt(sum_c + norm_eps), (128, 128)
                )
                rn[i, top : top + 128, :] = jnp.broadcast_to(
                    lax.rsqrt(sum_n + norm_eps), (128, 128)
                )

        weights_2(wcx, WC2)

        def attention(col, row, scale_ref, gains, tables, keep, out):
            q_ref, k_ref, v_ref = tables

            @pl.loop(0, NR)
            def _(i):
                rows = pl.ds(pl.multiple_of(i * ROWS, ROWS), ROWS)
                scale = scale_ref[i]
                cosine = cos[rows, :]
                sine = sin[rows, :]

                def raw(m):
                    block = pbuf[i, 0:ROWS, col + m * HEAD : col + (m + 1) * HEAD]
                    shift = pbuf[
                        i, ROWS + row : ROWS + row + 1, col + m * HEAD : col + (m + 1) * HEAD
                    ]
                    return scale * (block + shift)

                for m, (dst, raw_ref, inv_ref) in enumerate(
                    ((q_ref, qraw, invq), (k_ref, kraw, invk))
                ):
                    x = raw(m)
                    inverse = lax.rsqrt(jnp.mean(x * x, axis=1, keepdims=True) + norm_eps)
                    normed = x * inverse * gains[m : m + 1, :]
                    dst[rows, :] = (normed * cosine + half_turn(normed) * sine).astype(bf16)
                    if keep:
                        raw_ref[rows, :] = x
                        inv_ref[rows, :] = jnp.broadcast_to(inverse, (ROWS, HEAD))
                v_ref[rows, :] = raw(2).astype(bf16)

            @pl.loop(0, NR)
            def _(i):
                rows = pl.ds(pl.multiple_of(i * ROWS, ROWS), ROWS)
                exponent = jnp.exp(dot_nt(q_ref[rows, :], k_ref[...]) * score_scale)
                inverse = 1.0 / jnp.sum(exponent, axis=1, keepdims=True)
                if keep:
                    linv[rows, :] = jnp.broadcast_to(inverse, (ROWS, HEAD))
                prob = (exponent * inverse).astype(bf16)
                out(rows, dot(prob, v_ref[...]).astype(bf16))

        def to_a(rows, x):
            gt[rows, :] = x

        def to_fake(rows, x):
            fa[rows, :] = x

        def to_guided(rows, x):
            gt[rows, :] = (
                guidance * gt[rows, :].astype(f32) - (guidance - 1.0) * x.astype(f32)
            ).astype(bf16)

        attention(0, 0, rc, cqk, (qr, kr, vv), True, to_fake)
        tokens(fa, ac, EA)

        for n in range(2):
            other = pl.ds(pl.multiple_of((n * 2 + 1 - core) * ROWS, ROWS), ROWS)
            send(fa.at[other, :], pair.at[n, :, pl.ds(HEAD, HEAD)], FX, sibling)
            own = pl.ds(pl.multiple_of((n * 2 + core) * ROWS, ROWS), ROWS)
            pair[n, :, 0:HEAD] = fa[own, :]
        weights_2(wtx, WT2)
        for c in w_copies[4:]:
            c.wait()
        scale_w(tgain, 512, 768)

        @pl.loop(0, NR)
        def _(i):
            pbuf[i, :, 512:768] = dot(noisy[i], wall[:, 512:768])

        attention(384, 0, rc, tqk, (tq, tk, tv), False, to_a)
        attention(384, 1, rn, tqk, (tq, tk, tv), False, to_guided)
        tokens(gt, ag, EU)

    pl.run_scoped(
        forward_phase,
        pltpu.VMEM((D, 6 * HEAD), bf16),
        pltpu.VMEM((NR, BLK, 6 * HEAD), f32),
        pltpu.VMEM((LEN, HEAD), bf16),
        pltpu.VMEM((LEN, HEAD), bf16),
        pltpu.VMEM((LEN, HEAD), bf16),
    )

    fraction = (jnp.full((1, 128), scalars[0, 1], jnp.int32).astype(f32) + 1.0) / 1001.0
    noise = (5.0 * fraction / (1.0 + 4.0 * fraction))[:, 0:1]

    def later_phase(
        gaout, diff_out, fake, abs_out, qgopp, qgdir, qgkeep, qgsum, qgown, gk, gv, rgt,
        ogown, ogout,
    ):
        tile_cols = pl.ds(pl.multiple_of(myc * COLS, COLS), COLS)
        weights_3(wcx, WC3)
        wait_in(gen, EG)
        wait_in(ac, EA)
        wait_in(wcx.at[pl.ds(0, 16)], WC3)

        def predictions(i, total, guided):
            rows = pl.ds(pl.multiple_of(i * 128, 128), 128)
            latent = noisy[myr, rows, tile_cols].astype(f32)
            cond = latent + caps[0:1, tile_cols]
            if guided:
                null = latent + caps[1:2, tile_cols]
                velocity = guidance * cond - (guidance - 1.0) * null + total
            else:
                velocity = cond + total
            return latent - noise * velocity

        def product(att, weights, rows):
            return dot(att[rows, :], weights[...].reshape(NB * HEAD, COLS))

        def cotangent(i):
            rows = pl.ds(i * 128, 128)
            fake_pred = predictions(i, product(ac, wcx, rows), False)
            target = gen[rows, :].astype(f32)
            cotf[z_hi * 8 + s, rows, :] = (-noise * (fake_pred - target) * (1.0 / 64.0)).astype(bf16)
            fake[rows, :] = fake_pred

        cotangent(0)
        cotangent(1)

        @pl.loop(0, 8)
        def _(j):
            four = wcx[pl.ds(j * 4, 4)].reshape(4 * HEAD, COLS)
            part = dot_nt(cotf[z_hi * 8 + s], four)
            for m in range(4):
                gaout[j * 4 + m] = part[:, m * HEAD : (m + 1) * HEAD].astype(bf16)

        @pl.loop(1, NB)
        def _(k):
            q = peer(k)
            send(gaout.at[q], gain_in.at[me], EB, plane(q))

        local_in(gaout.at[me], gain_in.at[me], EB)

        top, low = pl.ds(0, 128), pl.ds(128, 128)
        chip = z_hi * 8 + s
        for k in (2, 1, 3):
            send(cotf.at[chip, top, :], cotf.at[chip, top, :], C1A, along_x(k))
            send(cotf.at[chip, low, :], cotf.at[chip, low, :], C1B, along_z(k))
        wait_in(cotf.at[pl.ds(0, 3), top, :], C1A)
        x_run = pl.ds(chip - x_at, 4)
        for k in (2, 1, 3):
            send(cotf.at[x_run, top, :], cotf.at[x_run, top, :], C2A, along_z(k))
        wait_in(cotf.at[pl.ds(0, 3), low, :], C1B)
        for k in (2, 1, 3):
            for z in range(4):
                held = cotf.at[z * 4 + x_at, low, :]
                send(held, held, C2B, along_x(k))
        wait_in(gain_in, EB)

        gk[...] = jnp.zeros_like(gk)
        gv[...] = jnp.zeros_like(gv)

        def undo(rows, raw_ref, inv_ref, gain, grad):
            turned = grad * cos[rows, :] + half_turn(grad * sin[rows, :])
            scaled = gain * turned
            raw = raw_ref[rows, :]
            inverse = inv_ref[rows, :]
            back = inverse * scaled - raw * inverse * inverse * inverse * jnp.mean(
                scaled * raw, axis=1, keepdims=True
            )
            return back.astype(bf16).astype(f32)

        @pl.loop(0, NR)
        def _(i):
            rows = pl.ds(pl.multiple_of(i * ROWS, ROWS), ROWS)
            total = jnp.zeros((ROWS, HEAD), f32)
            for c in range(8):
                total += gain_in[tile_of(i, c)].astype(f32)
            grads = total.astype(bf16)
            inverse = linv[rows, :][:, 0:1]
            prob = jnp.exp(dot_nt(qr[rows, :], kr[...]) * score_scale) * inverse
            grad_prob = dot_nt(grads, vv[...])
            mean = jnp.sum(grad_prob * prob, axis=1, keepdims=True)
            grad_score = (prob * (grad_prob - mean) * score_scale).astype(bf16)
            gq = dot(grad_score, kr[...])
            gk[...] += dot_tn(qr[rows, :], grad_score)
            gv[...] += dot_tn(grads, prob.astype(bf16))
            rg = rc[i] * undo(rows, qraw, invq, cqk[0:1, :], gq)
            rgt[0:HEAD, rows] = rg.T.astype(bf16)

        for i in range(NR):
            rows = pl.ds(i * ROWS, ROWS)
            grad_k = gk[:, i * ROWS : (i + 1) * ROWS].T
            grad_v = gv[:, i * ROWS : (i + 1) * ROWS].T
            grad_k = rc[i] * undo(rows, kraw, invk, cqk[1:2, :], grad_k)
            grad_v = rc[i] * grad_v.astype(bf16).astype(f32)
            rgt[HEAD : 2 * HEAD, rows] = grad_k.T.astype(bf16)
            rgt[2 * HEAD :, rows] = grad_v.T.astype(bf16)
        row_sum = jnp.sum(rgt[...].astype(f32), axis=1, keepdims=True)

        def share(target, put):
            @pl.loop(0, FEAT // 256)
            def _(j):
                cols = pl.ds(pl.multiple_of(target * FEAT + j * 256, 256), 256)
                total = row_sum * caps[0:1, cols]
                for i in range(NR):
                    total += dot(rgt[:, i * ROWS : (i + 1) * ROWS], noisy[i, 0:ROWS, cols])
                lines = cgain[pl.ds(target * (FEAT // 128) + j * 2, 2), :]
                gains = jnp.concatenate([lines[0:1], lines[1:2]], axis=1)
                put(pl.ds(pl.multiple_of(j * 256, 256), 256), total * gains)

        first, second = pl.ds(0, 192), pl.ds(192, 192)
        up, down = window(1), window(3)

        def put_opposite(cols, x):
            qgopp[0, :, cols] = x[0:192].astype(bf16)
            qgopp[1, :, cols] = x[192:384].astype(bf16)

        def put_up(cols, x):
            qgkeep[0, :, cols] = x[0:192]
            qgdir[0, :, cols] = x[192:384].astype(bf16)

        def put_down(cols, x):
            qgdir[1, :, cols] = x[0:192].astype(bf16)
            qgkeep[1, :, cols] = x[192:384]

        def put_own(cols, x):
            qgown[:, cols] = x

        share(lax.rem(w + 2, 4), put_opposite)
        send(qgopp.at[0], qgfwd.at[0], QF0, up)
        send(qgopp.at[1], qgfwd.at[1], QF1, down)
        share(lax.rem(w + 1, 4), put_up)
        send(qgdir.at[0], qgin.at[0, second, :], QD0, up)
        share(lax.rem(w + 3, 4), put_down)
        send(qgdir.at[1], qgin.at[1, first, :], QD1, down)
        share(w, put_own)
        wait_in(qgfwd.at[0], QF0)
        qgsum[0] = (qgkeep[0] + qgfwd[0].astype(f32)).astype(bf16)
        send(qgsum.at[0], qgin.at[0, first, :], QC0, up)
        wait_in(qgfwd.at[1], QF1)
        qgsum[1] = (qgkeep[1] + qgfwd[1].astype(f32)).astype(bf16)
        send(qgsum.at[1], qgin.at[1, second, :], QC1, down)

        weights_3(wtx, WT3)
        wait_in(ag, EU)
        wait_in(wtx.at[pl.ds(0, 16)], WT3)
        abs_out[...] = jnp.zeros_like(abs_out)

        @pl.loop(0, 2)
        def _(i):
            rows = pl.ds(pl.multiple_of(i * 128, 128), 128)
            real_pred = predictions(i, product(ag, wtx, rows), True)
            target = gen[rows, :].astype(f32)
            gap = jnp.abs(real_pred - target)
            lanes = gap[:, 0:128]
            for j in range(1, COLS // 128):
                lanes += gap[:, j * 128 : (j + 1) * 128]
            eight = lanes[0:8, :]
            for j in range(1, 16):
                eight += lanes[j * 8 : (j + 1) * 8, :]
            abs_out[...] += eight
            diff_out[rows, :] = (fake[rows, :] - real_pred).astype(bf16)

        @pl.loop(1, NB)
        def _(k):
            send(abs_out, abs_in.at[me], ES, plane(peer(k)))

        local_in(abs_out, abs_in.at[me], ES)

        diff_mine = diff_in.at[:, tile_cols]

        @pl.loop(0, 8)
        def _(t):
            e = lax.rem(t, 2)
            to_b = t // 2
            to_s = myr * 2 + e
            src = diff_out.at[pl.ds(pl.multiple_of(e * 128, 128), 128), :]
            mine = to_b * 8 + to_s == me

            @pl.when(mine)
            def _():
                local_in(src, diff_mine, ED)

            @pl.when(jnp.logical_not(mine))
            def _():
                send(src, diff_mine, ED, {"branch": to_b, "seq": to_s})

        wait_in(pair.at[:, :, pl.ds(0, HEAD)], FX)
        wait_in(cotf.at[pl.ds(0, 12), top, :], C2A)
        wait_in(cotf.at[pl.ds(0, 12), low, :], C2B)

        @pl.loop(0, 8)
        def _(c):
            base = (c // 4) * 8 + lax.rem(c, 4)
            total = dot_tn(pair[0], cotf[base]) + dot_tn(pair[1], cotf[base + 4])
            cols = pl.ds(pl.multiple_of(c * COLS, COLS), COLS)
            ogown[:, cols] = total[0:HEAD]
            ogout[:, cols] = total[HEAD:].astype(bf16)

        send(ogout, ogsib, CS, sibling)
        wait_in(ogsib, CS)
        wait_out(ogsib, CS)

        @pl.loop(0, 4)
        def _(n):
            cols = pl.ds(pl.multiple_of(n * FEAT, FEAT), FEAT)
            total = ogown[:, cols] + ogsib[:, cols].astype(f32)
            ogown[:, cols] = total
            ogout[:, cols] = total.astype(bf16)

        for off in (2, 1, 3):
            target = lax.rem(w + off, 4)
            shared = pl.ds(pl.multiple_of(target * FEAT, FEAT), FEAT)
            send(ogout.at[:, shared], og8in.at[off - 1], E8, {"rep": target})

        wait_in(abs_in, ES)
        wait_in(diff_in, ED)
        spread = jnp.sum(jnp.sum(abs_in[...], axis=0), axis=(0, 1), keepdims=True) * (
            1.0 / (LEN * D)
        )
        factor = 1.0 / (spread + 1e-05)

        @pl.loop(0, 8)
        def _(j):
            cols = pl.ds(pl.multiple_of(j * COLS, COLS), COLS)
            diff_in[:, cols] = (diff_in[:, cols].astype(f32) * factor).astype(bf16)

        gg_copy = local(diff_in, gg_h, lsem.at[17])

        wait_in(qgin.at[0, second, :], QD0)
        wait_in(qgin.at[1, first, :], QD1)
        wait_in(qgin.at[0, first, :], QC0)
        wait_in(qgin.at[1, second, :], QC1)

        def sum_q(out):
            copies = []
            for m in range(3):
                if m == 2:
                    copies[0].wait()
                for j in range(FEAT // 256):
                    rows = slice(m * HEAD, (m + 1) * HEAD)
                    cols = slice(j * 256, (j + 1) * 256)
                    total = qgown[rows, cols]
                    for way in range(2):
                        total += qgin[way, rows, cols].astype(f32)
                    out[m % 2, j * 256 : (j + 1) * 256, :] = total.T
                copies.append(local(out.at[m % 2], qg_h.at[m], lsem.at[4 + m]))
            copies[1].wait()
            copies[2].wait()

        pl.run_scoped(sum_q, pltpu.VMEM((2, FEAT, HEAD), f32))
        wait_in(og8in, E8)
        ogsum = ogown.at[:, pl.ds(pl.multiple_of(w * FEAT, FEAT), FEAT)]
        for j in range(5):
            cols = slice(j * 256, (j + 1) * 256)
            total = ogsum[:, cols]
            for off in range(3):
                total += og8in[off, :, cols].astype(f32)
            ogsum[:, cols] = total
        local(ogsum, og_h, lsem.at[19]).wait()
        gg_copy.wait()

        for dst, e in ((wcx, WC1), (wtx, WT1)):
            wait_out(dst.at[pl.ds(0, 15), pl.ds(0, 32), :], e)
            wait_out(dst.at[pl.ds(0, 16), pl.ds(0, 96), :], e + 1)
            wait_out(dst.at[pl.ds(0, 16)], e + 2)

        @pl.when(has_rows)
        def _():
            wait_out(diff_in.at[:, pl.ds(0, 3 * COLS)], EG)

        wait_out(ac.at[:, pl.ds(0, (NB - 1) * HEAD)], EA)
        wait_out(ag.at[:, pl.ds(0, (NB - 1) * HEAD)], EU)
        wait_out(cotf.at[pl.ds(0, 3), top, :], C1A)
        wait_out(cotf.at[pl.ds(0, 3), low, :], C1B)
        wait_out(cotf.at[pl.ds(0, 12), top, :], C2A)
        wait_out(cotf.at[pl.ds(0, 12), low, :], C2B)
        wait_out(pair.at[:, :, pl.ds(0, HEAD)], FX)
        wait_out(gain_in.at[pl.ds(0, NB - 1)], EB)
        wait_out(abs_in.at[pl.ds(0, NB - 1)], ES)

        @pl.when(has_rows)
        def _():
            wait_out(diff_in.at[:, pl.ds(0, 7 * COLS)], ED)

        @pl.when(jnp.logical_not(has_rows))
        def _():
            wait_out(diff_in, ED)

        for way, e in ((0, QF0), (1, QF1), (0, QD0), (1, QD1), (0, QC0), (1, QC1)):
            wait_out(qgfwd.at[way], e)
        wait_out(og8in, E8)

    pl.run_scoped(
        later_phase,
        pltpu.VMEM((NB, ROWS, HEAD), bf16),
        pltpu.VMEM((ROWS, COLS), bf16),
        pltpu.VMEM((ROWS, COLS), f32),
        pltpu.VMEM((8, 128), f32),
        pltpu.VMEM((2, 192, FEAT), bf16),
        pltpu.VMEM((2, 192, FEAT), bf16),
        pltpu.VMEM((2, 192, FEAT), f32),
        pltpu.VMEM((2, 192, FEAT), bf16),
        pltpu.VMEM((3 * HEAD, FEAT), f32),
        pltpu.VMEM((HEAD, LEN), f32),
        pltpu.VMEM((HEAD, LEN), f32),
        pltpu.VMEM((3 * HEAD, LEN), bf16),
        pltpu.VMEM((HEAD, D), f32),
        pltpu.VMEM((HEAD, D), bf16),
    )


def body(
    noisy, generated, caption, null_caption, caption_drop, timestep, window_start,
    teacher_qkv, teacher_out, teacher_gain, teacher_qk_gain,
    critic_qkv, critic_out, critic_gain, critic_qk_gain,
):
    scalars = jnp.stack([caption_drop, timestep, window_start], axis=1)
    hbm = pl.BlockSpec(memory_space=pl.ANY)
    vmem = pl.BlockSpec(memory_space=pltpu.VMEM)
    gg, qg, og = pl.pallas_call(
        step_kernel,
        name="generator_step",
        out_shape=(
            jax.ShapeDtypeStruct((128, D), bf16),
            jax.ShapeDtypeStruct((3, FEAT, HEAD), f32),
            jax.ShapeDtypeStruct((HEAD, FEAT), f32),
        ),
        in_specs=[pl.BlockSpec(memory_space=pltpu.SMEM)] + [hbm] * 3 + [vmem] * 7 + [hbm] * 3,
        out_specs=(hbm, hbm, hbm),
        scratch_shapes=[
            pltpu.VMEM((NR, BLK, D), bf16),
            pltpu.VMEM((NB, HEAD, COLS), bf16),
            pltpu.VMEM((NB, HEAD, COLS), bf16),
            pltpu.VMEM((ROWS, NB * HEAD), bf16),
            pltpu.VMEM((ROWS, NB * HEAD), bf16),
            pltpu.VMEM((NB, ROWS, HEAD), bf16),
            pltpu.VMEM((NB // 2, ROWS, COLS), bf16),
            pltpu.VMEM((2, ROWS, 2 * HEAD), bf16),
            pltpu.VMEM((HEAD, D), bf16),
            pltpu.VMEM((2, 3 * HEAD, FEAT), bf16),
            pltpu.VMEM((2, 192, FEAT), bf16),
            pltpu.VMEM((3, HEAD, FEAT), bf16),
            pltpu.VMEM((128, D), bf16),
            pltpu.VMEM((NB, 8, 128), f32),
            pltpu.VMEM((ROWS, COLS), bf16),
            pltpu.VMEM((LEN, HEAD), f32),
            pltpu.VMEM((LEN, HEAD), f32),
            pltpu.VMEM((8, D), f32),
            pltpu.VMEM((LEN, HEAD), f32),
            pltpu.VMEM((LEN, HEAD), f32),
            pltpu.VMEM((LEN, HEAD), bf16),
            pltpu.VMEM((LEN, HEAD), bf16),
            pltpu.VMEM((LEN, HEAD), bf16),
            pltpu.VMEM((NR, ROWS, HEAD), f32),
            pltpu.VMEM((NR, ROWS, HEAD), f32),
            pltpu.VMEM((LEN, HEAD), f32),
            pltpu.VMEM((LEN, HEAD), f32),
            pltpu.VMEM((LEN, HEAD), f32),
            pltpu.VMEM((LEN, HEAD), bf16),
            pltpu.VMEM((LEN, HEAD), bf16),
            pltpu.SemaphoreType.DMA((20,)),
            pltpu.SemaphoreType.DMA((25,)),
            pltpu.SemaphoreType.DMA((25,)),
        ],
        compiler_params=pltpu.CompilerParams(
            collective_id=0, has_side_effects=True, vmem_limit_bytes=127 * 512 * 1024
        ),
    )(
        scalars, noisy[0], critic_qkv, teacher_qkv,
        caption.reshape(40, 128).astype(f32), null_caption.reshape(40, 128).astype(f32),
        rope_table(), critic_qk_gain, teacher_qk_gain,
        critic_gain.reshape(40, 128), teacher_gain.reshape(40, 128),
        generated[0], critic_out, teacher_out,
    )
    return (gg[None], qg, og)


def solution(mesh):
    in_specs = (
        P("rep", None, None),
        P("rep", "seq", None),
        P("rep", None),
        P(),
        P("rep"),
        P("rep"),
        P("rep"),
        P(None, None, ("branch", "seq")),
        P(("branch", "seq"), None),
        P(),
        P(None, ("branch", "seq")),
        P(None, None, ("branch", "seq")),
        P(("branch", "seq"), None),
        P(),
        P(None, ("branch", "seq")),
    )
    out_specs = (
        P("rep", "seq", None),
        P(None, "rep", ("branch", "seq")),
        P(("branch", "seq"), "rep"),
    )
    return jax.shard_map(body, mesh=mesh, in_specs=in_specs, out_specs=out_specs, check_vma=False)
```
